512 devices in a mesh: ctx: 64 (over z, y), head: 8 (over x, core).
Axes of the slice: x: 4, y: 4, z: 16, core: 2. Of those that a mesh axis runs over, the one named last changes fastest.
Arguments:
- query_lin: bfloat16 [8192, 256], P('ctx', 'head'), may hold values from -4 to 4
- key_lin: bfloat16 [8192, 256], P('ctx', 'head'), may hold values from -4 to 4
- values: bfloat16 [8192, 2048], P('ctx', 'head'), may hold values from -24 to 24
- win_queries: bfloat16 [8192, 2048], P('ctx', 'head'), may hold values from -6 to 6
- win_keys: bfloat16 [8192, 2048], P('ctx', 'head'), may hold values from -6 to 6
- gain: float32 [2048], P('head'), may hold values from 0.1 to 1.9
- grad_out: bfloat16 [8192, 2048], P('ctx', 'head'), may hold values from -6 to 6
Outputs:
- mixed_out: bfloat16 [8192, 2048], P('ctx', 'head')
- grad_query_lin: bfloat16 [8192, 256], P('ctx', 'head')
- grad_key_lin: bfloat16 [8192, 256], P('ctx', 'head')
- grad_values: bfloat16 [8192, 2048], P('ctx', 'head')
- grad_win_queries: bfloat16 [8192, 2048], P('ctx', 'head')
- grad_win_keys: bfloat16 [8192, 2048], P('ctx', 'head')
The draws below stay inside these ranges and needn't reach their ends.
All inputs are finite; a program needn't handle non-finite values.
Results may differ from the reference program's by a relative error of at most 0.015.
Values may be sent and summed in bfloat16 or wider, within the bound.
A program may use at most 128 MiB of HBM per device.

```python
import math
import jax
import jax.numpy as jnp
from jax import lax

HEADS = 16
KD = 16
DV = 128
WD = 128
WINDOW = 128
TOK_DEV = 128
FEAT = 273
TOKENS = 8192


def window_pair(key):
    full_width = HEADS * WD
    base_q = jnp.clip(jax.random.normal(jax.random.fold_in(key, 11), (TOKENS, full_width), jnp.float32), -4.0, 4.0)
    base_k = jnp.clip(jax.random.normal(jax.random.fold_in(key, 12), (TOKENS, full_width), jnp.float32), -4.0, 4.0)
    query_draw = base_q
    key_draw = base_k
    return (query_draw, key_draw)


def draw_win_queries(key, part):
    return window_pair(key)[0].astype(jnp.bfloat16)


def draw_win_keys(key, part):
    return window_pair(key)[1].astype(jnp.bfloat16)


def draw_values(key, part):
    full_width = HEADS * DV
    col_frac = jnp.arange(full_width, dtype=jnp.float32) / (full_width - 1)
    spread = jnp.exp(jax.random.uniform(jax.random.fold_in(key, 21), (full_width,), jnp.float32, math.log(0.3), math.log(3.0)))
    base = jnp.clip(jax.random.normal(jax.random.fold_in(key, 22), (TOKENS, full_width), jnp.float32), -3.0, 3.0)
    rise_col = 1.0 + 0.9 * col_frac
    return (base * spread * rise_col).astype(jnp.bfloat16)


def level_of(stream_key, extent, shards, least, largest):
    level = 1.0
    for axis_at, parts in shards:
        steps = jax.random.uniform(jax.random.fold_in(jax.random.fold_in(stream_key, 6), axis_at), (parts,), jnp.float32, least / len(shards), largest / len(shards))
        level = level * jnp.repeat(jnp.exp(steps), extent[axis_at] // parts).reshape((-1,) + (1,) * (len(extent) - 1 - axis_at))
    return level


def scatter_about(rng, extent, deviation, limit, shards=(), kind=jnp.bfloat16):
    drawn = deviation * jax.random.normal(rng, extent, jnp.float32)
    if shards:
        drawn = drawn * level_of(rng, extent, shards, -0.22, 0.18)
    return jnp.clip(drawn, -limit, limit).astype(kind)


def setup_inputs(seed: int = 0) -> dict:
    key_list = jax.random.split(jax.random.key(seed), 8)
    return {
        "query_lin": scatter_about(key_list[0], (TOKENS, HEADS * KD), 1.0, 4.0, ((0, 64), (1, 8))),
        "key_lin": scatter_about(key_list[1], (TOKENS, HEADS * KD), 1.0, 4.0, ((0, 64), (1, 8))),
        "values": draw_values(jax.random.fold_in(key_list[7], 71), 0),
        "win_queries": draw_win_queries(jax.random.fold_in(key_list[7], 71), 0),
        "win_keys": draw_win_keys(jax.random.fold_in(key_list[7], 71), 0),
        "gain": jnp.clip(1.0 + 0.18 * jax.random.normal(key_list[5], (HEADS * DV,), jnp.float32), 0.1, 1.9),
        "grad_out": scatter_about(key_list[6], (TOKENS, HEADS * DV), 1.0, 6.0, ((0, 64), (1, 8))),
    }


epsilon = 1e-06

def features(points):
    key_depth = points.shape[-1]
    linear_part = points / math.sqrt(math.sqrt(key_depth))
    outer_part = (points[..., :, None] * points[..., None, :]).reshape(points.shape[:-1] + (key_depth * key_depth,))
    outer_part = outer_part / (math.sqrt(2.0) * math.sqrt(key_depth))
    return jnp.concatenate([jnp.ones_like(points[..., :1]), linear_part, outer_part], axis=-1)

def rounded(array):
    return lax.optimization_barrier(array.astype(jnp.bfloat16)).astype(jnp.float32)

def window_math(query_blk, key_blk, value_blk, dout_blk, allowed, scale_win):
    query_f = query_blk.astype(jnp.float32)
    key_f = key_blk.astype(jnp.float32)
    value_f = value_blk.astype(jnp.float32)
    dout_f = dout_blk.astype(jnp.float32)
    scores = jnp.einsum('the,she->hts', query_f, key_f) * scale_win
    row_top = lax.optimization_barrier(jnp.max(jnp.where(allowed, scores, -jnp.inf), axis=-1, keepdims=True))
    weights = jnp.where(allowed, jnp.exp(scores - row_top), 0.0)
    row_total = lax.optimization_barrier(jnp.sum(weights, axis=-1, keepdims=True))
    soft_probs = weights / row_total
    probs_round = rounded(soft_probs)
    win_out = jnp.einsum('hts,shd->thd', probs_round, value_f)
    grad_prob = jnp.einsum('thd,shd->hts', dout_f, value_f)
    row_delta = jnp.swapaxes(lax.optimization_barrier(jnp.sum(dout_f * win_out, axis=-1)), -1, -2)[..., None]
    grad_score = rounded(soft_probs * (grad_prob - row_delta))
    grad_query = jnp.einsum('hts,she->the', grad_score, key_f) * scale_win
    grad_keys = jnp.einsum('hts,the->she', grad_score, query_f) * scale_win
    grad_vals = jnp.einsum('hts,thd->shd', probs_round, dout_f)
    return (win_out, grad_query, grad_keys, grad_vals)

def reference(query_lin, key_lin, values, win_queries, win_keys, gain, grad_out):
    full_width = HEADS * DV
    scale_lin = 1.0 / math.sqrt(KD)
    scale_win = 1.0 / math.sqrt(WD)
    win_count = TOKENS // WINDOW
    key_pad = jnp.concatenate([jnp.zeros((WINDOW, HEADS * WD), win_keys.dtype), win_keys], axis=0)
    value_pad = jnp.concatenate([jnp.zeros((WINDOW, full_width), values.dtype), values], axis=0)
    row_pos = jnp.arange(WINDOW, dtype=jnp.int32)[:, None]
    col_pos = jnp.arange(2 * WINDOW, dtype=jnp.int32)[None, :]
    band_mask = (col_pos > row_pos) & (col_pos <= row_pos + WINDOW)

    def window_block(block_index):
        row_start = (block_index * WINDOW).astype(jnp.int32)
        query_blk = lax.dynamic_slice_in_dim(win_queries, row_start, WINDOW, 0).reshape(WINDOW, HEADS, WD)
        key_blk = lax.dynamic_slice_in_dim(key_pad, row_start, 2 * WINDOW, 0).reshape(2 * WINDOW, HEADS, WD)
        value_blk = lax.dynamic_slice_in_dim(value_pad, row_start, 2 * WINDOW, 0).reshape(2 * WINDOW, HEADS, DV)
        dout_blk = lax.dynamic_slice_in_dim(grad_out, row_start, WINDOW, 0).reshape(WINDOW, HEADS, DV)
        allowed = (band_mask & (row_start - WINDOW + col_pos >= 0))[None]
        win_out, grad_query, grad_keys, grad_vals = window_math(query_blk, key_blk, value_blk, dout_blk, allowed, scale_win)
        return (win_out.reshape(WINDOW, full_width), grad_query.reshape(WINDOW, HEADS * WD).astype(jnp.bfloat16), grad_keys, grad_vals)
    window_parts = lax.map(window_block, jnp.arange(win_count, dtype=jnp.int32))
    key_grads_all = window_parts[2]
    value_grads_all = window_parts[3]
    key_spill = jnp.concatenate([key_grads_all[1:, :WINDOW], jnp.zeros((1, WINDOW, HEADS, WD), key_grads_all.dtype)], axis=0)
    value_spill = jnp.concatenate([value_grads_all[1:, :WINDOW], jnp.zeros((1, WINDOW, HEADS, DV), value_grads_all.dtype)], axis=0)
    key_own = key_grads_all[:, WINDOW:] + key_spill
    value_own = value_grads_all[:, WINDOW:] + value_spill
    window_out = window_parts[0].reshape(TOKENS, full_width)
    grad_win_queries = window_parts[1].reshape(TOKENS, HEADS * WD)
    grad_win_keys = key_own.reshape(TOKENS, HEADS * WD).astype(jnp.bfloat16)
    value_window = value_own.reshape(TOKENS, full_width)
    blocks = TOKENS // TOK_DEV
    query_blocks = query_lin.reshape(blocks, TOK_DEV, HEADS, KD)
    key_blocks = key_lin.reshape(blocks, TOK_DEV, HEADS, KD)
    value_blocks = values.reshape(blocks, TOK_DEV, HEADS, DV)
    dout_blocks = grad_out.reshape(blocks, TOK_DEV, full_width)
    window_blocks = window_out.reshape(blocks, TOK_DEV, full_width)
    causal = jnp.tril(jnp.ones((TOK_DEV, TOK_DEV), jnp.bool_))

    def local_terms(query_blk, key_blk, value_blk, grad_lin):
        query_f = query_blk.astype(jnp.float32)
        key_f = key_blk.astype(jnp.float32)
        lin_score = jnp.einsum('thk,shk->hts', query_f, key_f) * scale_lin
        kernel = rounded(jnp.where(causal, 1.0 + lin_score + 0.5 * lin_score * lin_score, 0.0))
        value_dot = jnp.einsum('thd,shd->hts', grad_lin, value_blk.astype(jnp.float32))
        grad_score = rounded(jnp.where(causal, value_dot * (1.0 + lin_score), 0.0))
        return (query_f, key_f, lin_score, kernel, grad_score)

    def forward_step(prefix, pieces):
        query_blk, key_blk, value_blk, dout_blk, window_blk = pieces
        query_f = query_blk.astype(jnp.float32)
        key_f = key_blk.astype(jnp.float32)
        value_f = value_blk.astype(jnp.float32)
        query_feat, pull_query = jax.vjp(features, query_f)
        query_phi = rounded(query_feat)
        key_phi = rounded(features(key_f))
        lin_score = jnp.einsum('thk,shk->hts', query_f, key_f) * scale_lin
        kernel = rounded(jnp.where(causal, 1.0 + lin_score + 0.5 * lin_score * lin_score, 0.0))
        prefix_round = rounded(prefix)
        linear_out = jnp.einsum('hts,shd->thd', kernel, value_f) + jnp.einsum('thf,hfd->thd', query_phi, prefix_round)
        linear_flat = linear_out.reshape(TOK_DEV, full_width)
        dout_f = dout_blk.astype(jnp.float32)
        inverse = (1.0 / jnp.sqrt(lax.optimization_barrier(jnp.sum(linear_flat * linear_flat, axis=1)) / full_width + epsilon))[:, None]
        mixed_blk = (linear_flat * inverse * gain + window_blk).astype(jnp.bfloat16)
        cross = (lax.optimization_barrier(jnp.sum(gain * dout_f * linear_flat, axis=1)) / full_width)[:, None]
        grad_lin = rounded(inverse * gain * dout_f - linear_flat * inverse * inverse * inverse * cross)
        grad_lin_h = grad_lin.reshape(TOK_DEV, HEADS, DV)
        value_dot = jnp.einsum('thd,shd->hts', grad_lin_h, value_f)
        grad_score = rounded(jnp.where(causal, value_dot * (1.0 + lin_score), 0.0))
        query_pull = jnp.einsum('thd,hfd->thf', grad_lin_h, prefix_round)
        grad_query = jnp.einsum('hts,shk->thk', grad_score, key_f) * scale_lin + pull_query(query_pull)[0]
        local_state = jnp.einsum('shf,shd->hfd', key_phi, value_f)
        return (prefix + local_state, (mixed_blk, grad_lin_h.astype(jnp.bfloat16), grad_query.astype(jnp.bfloat16)))
    state_zero = jnp.zeros((HEADS, FEAT, DV), jnp.float32)
    state_end, forward_parts = lax.scan(forward_step, state_zero, (query_blocks, key_blocks, value_blocks, dout_blocks, window_blocks))
    mixed_out = forward_parts[0].reshape(TOKENS, full_width)
    grad_lin_blocks = forward_parts[1]
    grad_query_lin = forward_parts[2].reshape(TOKENS, HEADS * KD)

    def backward_step(suffix, pieces):
        query_blk, key_blk, value_blk, grad_lin_b = pieces
        grad_lin = grad_lin_b.astype(jnp.float32)
        query_f, key_f, lin_score, kernel, grad_score = local_terms(query_blk, key_blk, value_blk, grad_lin)
        value_f = value_blk.astype(jnp.float32)
        query_phi = rounded(features(query_f))
        key_feat, pull_key = jax.vjp(features, key_f)
        key_phi = rounded(key_feat)
        suffix_round = rounded(suffix)
        grad_value_lin = jnp.einsum('hts,thd->shd', kernel, grad_lin) + jnp.einsum('shf,hfd->shd', key_phi, suffix_round)
        key_pull = jnp.einsum('shd,hfd->shf', value_f, suffix_round)
        grad_key = jnp.einsum('hts,thk->shk', grad_score, query_f) * scale_lin + pull_key(key_pull)[0]
        local_back = jnp.einsum('thf,thd->hfd', query_phi, grad_lin)
        return (suffix + local_back, (grad_key.astype(jnp.bfloat16), grad_value_lin))
    suffix_end, backward_parts = lax.scan(backward_step, state_zero, (query_blocks, key_blocks, value_blocks, grad_lin_blocks), reverse=True)
    grad_key_lin = backward_parts[0].reshape(TOKENS, HEADS * KD)
    grad_values = (backward_parts[1].reshape(TOKENS, full_width) + value_window).astype(jnp.bfloat16)
    return (mixed_out, grad_query_lin, grad_key_lin, grad_values, grad_win_queries, grad_win_keys)
```

```python
import math

import jax
import jax.numpy as jnp
import numpy as np
from jax import lax
from jax.experimental import pallas as pl
from jax.experimental.pallas import tpu as pltpu
from jax.sharding import PartitionSpec as P

HEADS = 16
KD = 16
DV = 128
WD = 128
TOK = 128
NY = 4
NZ = 16
NH = 8
ROWS = 160
HALF = ROWS // 2
WIDTH = HEADS * DV
EPS = 1e-06
MESH = pl.DeviceIdType.MESH
BF = jnp.bfloat16
F32 = jnp.float32


def selectors():
    first = np.zeros((2 * ROWS, 2 * KD), np.float32)
    second = np.zeros((2 * ROWS, 2 * KD), np.float32)
    for h in range(2):
        base, lane = h * ROWS, h * KD
        for i in range(KD):
            first[base + 1 + i, lane + i] = 1
            first[base + 17 + i, lane + i] = 1
            second[base + 17 + i, lane + i] = 1
        row = base + 33
        for i in range(KD):
            for j in range(i + 1, KD):
                first[row, lane + i] = 1
                second[row, lane + j] = 1
                row += 1
    return first, second


def nn(a, b):
    return lax.dot_general(a, b, (((1,), (0,)), ((), ())), preferred_element_type=F32)


def nt(a, b):
    return lax.dot_general(a, b, (((1,), (1,)), ((), ())), preferred_element_type=F32)


def tn(a, b):
    return lax.dot_general(a, b, (((0,), (0,)), ((), ())), preferred_element_type=F32)


def kernel(
    ql_ref, kl_ref, v_ref, wq_ref, wk_ref, gain_ref, do_ref, e1_ref, e2_ref,
    mixed_ref, gql_ref, gkl_ref, gv_ref, gwq_ref, gwk_ref,
    krim, vrim, gkout, gvout, gkin, gvin,
    st_a, r1_a, t_a, rz_a, w_a, rw_a, out_a, pre_a,
    st_b, r1_b, t_b, rz_b, w_b, rw_b, out_b, pre_b,
    sums, sums_in, lin_sc, win_sc, ker_sc, gvacc, gkacc, phiq_sc, phik_sc,
    ss, rs,
):
    ctx = lax.axis_index("ctx")
    head = lax.axis_index("head")
    z = ctx // NY
    y = lax.rem(ctx, NY)
    sends = []

    def at(zz, yy):
        return {"ctx": lax.rem(zz + NZ, NZ) * NY + lax.rem(yy + NY, NY)}

    ahead = {"ctx": lax.rem(ctx + 1, NZ * NY)}
    behind = {"ctx": lax.rem(ctx + NZ * NY - 1, NZ * NY)}

    barrier = pltpu.get_barrier_semaphore()
    peers = [at(z, y + d) for d in (1, 2, 3)]
    peers += [at(z + d, y) for d in (1, 2, 3, 4, 8, -4, -3, -2, -1)]
    peers += [ahead, behind]
    peers += [{"head": lax.rem(head + d, NH)} for d in range(1, NH)]
    for peer in peers:
        pl.semaphore_signal(barrier, inc=1, device_id=peer, device_id_type=MESH)

    def send(src, dst, slot, device):
        copy = pltpu.make_async_remote_copy(
            src_ref=src, dst_ref=dst, send_sem=ss.at[slot], recv_sem=rs.at[slot],
            device_id=device, device_id_type=MESH,
        )
        copy.start()
        sends.append(copy)
        return copy

    def wait_all(copies):
        for copy in copies:
            copy.wait_recv()

    def flag(cond):
        return jnp.where(cond, 1.0, 0.0).astype(F32)

    class Scan:
        def __init__(self, sign, base, st, r1, t, rz, w, rw, out, pre):
            self.sign, self.base = sign, base
            self.st, self.r1, self.t, self.rz = st, r1, t, rz
            self.w, self.rw, self.out, self.pre = w, rw, out, pre

        def start(self):
            self.c1 = [
                send(self.st.at[lax.rem(y + d, NY)], self.r1.at[d - 1], self.base + d - 1, at(z, y + d))
                for d in (1, 2, 3)
            ]

        def parts(self):
            return [self.st[y].astype(F32)] + [self.r1[d].astype(F32) for d in range(3)]

        def rows(self):
            wait_all(self.c1)
            p = self.parts()
            self.t[...] = ((p[0] + p[1]) + (p[2] + p[3])).astype(BF)
            self.c2 = [
                send(self.t, self.rz.at[j - 1], self.base + 2 + j, at(z + self.sign * j, y))
                for j in (1, 2, 3)
            ]

        def holds(self, j):
            return flag(z - j >= 0) if self.sign > 0 else flag(z + j < NZ)

        def near(self):
            total = self.rz[0].astype(F32) * self.holds(1)
            for j in (2, 3):
                total = total + self.rz[j - 1].astype(F32) * self.holds(j)
            return total

        def windows(self):
            wait_all(self.c2)
            p = self.parts()
            self.w[...] = ((p[0] + p[1]) + (p[2] + p[3]) + self.near()).astype(BF)
            self.c3 = [
                send(self.w, self.rw.at[j - 1], self.base + 5 + j, at(z + self.sign * 4 * j, y))
                for j in (2, 1, 3)
            ]

        def spread(self):
            wait_all(self.c3)
            total = self.near()
            for j in (1, 2, 3):
                total = total + self.rw[j - 1].astype(F32) * self.holds(4 * j)
            p = self.parts()
            self.c4 = []
            for e in (2, 1, 3, 0):
                dest = lax.rem(y + e, NY)
                mine = total
                for d in range(NY):
                    source = lax.rem(y + NY - d, NY)
                    earlier = source < dest if self.sign > 0 else source > dest
                    mine = mine + p[d] * flag(earlier)
                if e == 0:
                    self.pre[y] = mine.astype(BF)
                else:
                    self.out[e - 1] = mine.astype(BF)
                    self.c4.append(
                        send(self.out.at[e - 1], self.pre.at[y], self.base + 8 + e, at(z, y + e))
                    )

        def finish(self):
            wait_all(self.c4)

    fwd = Scan(1, 0, st_a, r1_a, t_a, rz_a, w_a, rw_a, out_a, pre_a)
    bwd = Scan(-1, 12, st_b, r1_b, t_b, rz_b, w_b, rw_b, out_b, pre_b)

    lane32 = lax.broadcasted_iota(jnp.int32, (TOK, 2 * KD), 1)
    row = lax.broadcasted_iota(jnp.int32, (TOK, TOK), 0)
    col = lax.broadcasted_iota(jnp.int32, (TOK, TOK), 1)
    causal = col <= row
    frow = lax.broadcasted_iota(jnp.int32, (ROWS, TOK), 0)
    add_first = jnp.where(frow == 0, 1.0, 0.0)
    add_second = jnp.where(frow <= KD, 1.0, 0.0)
    pair_scale = 1.0 / (math.sqrt(2.0) * math.sqrt(KD))
    scale = jnp.where(frow == 0, 1.0, jnp.where(frow <= KD, 1.0 / math.sqrt(math.sqrt(KD)), pair_scale))
    weight = jnp.where(frow >= 33, 2.0, 1.0)

    def factors(x, h):
        rows = slice(h * ROWS, (h + 1) * ROWS)
        return nt(e1_ref[rows, :], x) + add_first, nt(e2_ref[rows, :], x) + add_second

    def phi(x, h):
        a, b = factors(x, h)
        return (a * b * scale).astype(BF)

    def heavy(features):
        return (features.astype(F32) * weight).astype(BF)

    def pull(x, h, cot):
        a, b = factors(x, h)
        rows = slice(h * ROWS, (h + 1) * ROWS)
        cot = cot * (scale * weight)
        return tn((cot * b).astype(BF), e1_ref[rows, :]) + tn((cot * a).astype(BF), e2_ref[rows, :])

    def own(x, h):
        inside = (lane32 >= h * KD) & (lane32 < (h + 1) * KD)
        return jnp.where(inside, x.astype(F32), 0.0).astype(BF)

    cols = [slice(h * DV, (h + 1) * DV) for h in range(2)]
    ql, kl = ql_ref[...], kl_ref[...]

    for h in range(2):
        key_phi = phi(kl, h)
        phik_sc[h] = key_phi
        state = nn(key_phi, v_ref[:, cols[h]])
        st_a[2 * h] = state[:HALF].astype(BF)
        st_a[2 * h + 1] = state[HALF:].astype(BF)

    pl.semaphore_wait(barrier, len(peers))
    fwd.start()
    rim = [
        send(wk_ref, krim, 24, ahead),
        send(v_ref, vrim, 25, ahead),
    ]

    def lin_score(h):
        return nt(own(ql, h), kl) * (1.0 / math.sqrt(KD))

    for h in range(2):
        phiq_sc[h] = phi(ql, h)
        s = lin_score(h)
        ker = jnp.where(causal, 1.0 + s + 0.5 * s * s, 0.0).astype(BF)
        ker_sc[h] = ker
        lin_sc[:, cols[h]] = nn(ker, v_ref[:, cols[h]])

    fwd.rows()

    scale_win = 1.0 / math.sqrt(WD)
    edge = (col > row) & (ctx > 0)
    wait_all(rim)

    def window(h):
        c = cols[h]
        q, k1, k2 = wq_ref[:, c], krim[:, c], wk_ref[:, c]
        v1, v2, do = vrim[:, c], v_ref[:, c], do_ref[:, c]
        s1 = jnp.where(edge, nt(q, k1) * scale_win, -1e30)
        s2 = jnp.where(causal, nt(q, k2) * scale_win, -1e30)
        top = jnp.maximum(
            jnp.max(s1, axis=1, keepdims=True), jnp.max(s2, axis=1, keepdims=True)
        )
        x1 = jnp.where(edge, jnp.exp(s1 - top), 0.0)
        x2 = jnp.where(causal, jnp.exp(s2 - top), 0.0)
        inv = 1.0 / (jnp.sum(x1, axis=1, keepdims=True) + jnp.sum(x2, axis=1, keepdims=True))
        p1, p2 = x1 * inv, x2 * inv
        b1, b2 = p1.astype(BF), p2.astype(BF)
        out = nn(b1, v1) + nn(b2, v2)
        win_sc[:, c] = out
        delta = jnp.sum(do.astype(F32) * out, axis=1, keepdims=True)
        g1 = (p1 * (nt(do, v1) - delta)).astype(BF)
        g2 = (p2 * (nt(do, v2) - delta)).astype(BF)
        gkout[:, c] = (tn(g1, q) * scale_win).astype(BF)
        gvout[:, c] = tn(b1, do).astype(BF)
        gwq_ref[:, c] = ((nn(g1, k1) + nn(g2, k2)) * scale_win).astype(BF)
        gkacc[:, c] = tn(g2, q) * scale_win
        gvacc[:, c] = tn(b2, do)

    window(0)
    fwd.windows()
    window(1)
    fwd.spread()
    back = [
        send(gkout, gkin, 26, behind),
        send(gvout, gvin, 27, behind),
    ]
    fwd.finish()

    gain = gain_ref[...]
    for h in range(2):
        prefix = pre_a[2 * h : 2 * h + 2].reshape(ROWS, DV)
        lin_sc[:, cols[h]] += tn(heavy(phiq_sc[h]), prefix)
    lin = lin_sc[...]
    gd = gain * do_ref[...].astype(F32)
    square = jnp.sum(lin * lin, axis=1, keepdims=True)
    cross = jnp.sum(gd * lin, axis=1, keepdims=True)
    both = jnp.where(col == 0, square, jnp.where(col == 1, cross, 0.0))
    sums[...] = both.T[:8]
    shares = [
        send(sums, sums_in.at[d - 1], 27 + d, {"head": lax.rem(head + d, NH)})
        for d in range(1, NH)
    ]
    wait_all(shares)
    total = sums[...]
    for d in range(NH - 1):
        total = total + sums_in[d]
    total = jnp.concatenate([total, jnp.zeros((TOK - 8, TOK), F32)], axis=0).T
    square = jnp.sum(jnp.where(col == 0, total, 0.0), axis=1, keepdims=True)
    cross = jnp.sum(jnp.where(col == 1, total, 0.0), axis=1, keepdims=True)
    inverse = 1.0 / jnp.sqrt(square * (1.0 / WIDTH) + EPS)
    grad_lin = (
        inverse * gd - lin * (inverse * inverse * inverse * (cross * (1.0 / WIDTH)))
    ).astype(BF)
    for h in range(2):
        state = nn(phiq_sc[h], grad_lin[:, cols[h]])
        st_b[2 * h] = state[:HALF].astype(BF)
        st_b[2 * h + 1] = state[HALF:].astype(BF)
    bwd.start()
    mixed_ref[...] = (lin * inverse * gain + win_sc[...]).astype(BF)

    gq = jnp.zeros((TOK, 2 * KD), F32)
    gk = jnp.zeros((TOK, 2 * KD), F32)
    for h in range(2):
        gl = grad_lin[:, cols[h]]
        g = nt(gl, v_ref[:, cols[h]]) * (1.0 + lin_score(h))
        g = jnp.where(causal, g, 0.0).astype(BF)
        gq = gq + nn(g, own(kl, h)) * (1.0 / math.sqrt(KD))
        gk = gk + tn(g, own(ql, h)) * (1.0 / math.sqrt(KD))
        if h == 0:
            bwd.rows()
    for h in range(2):
        gl = grad_lin[:, cols[h]]
        prefix = pre_a[2 * h : 2 * h + 2].reshape(ROWS, DV)
        gq = gq + pull(ql, h, nt(prefix, gl))
        gvacc[:, cols[h]] += tn(ker_sc[h], gl)
    gql_ref[...] = gq.astype(BF)
    bwd.windows()
    wait_all(back)
    gwk_ref[...] = (gkacc[...] + gkin[...].astype(F32)).astype(BF)
    gvacc[...] += gvin[...].astype(F32)
    bwd.spread()
    bwd.finish()
    for h in range(2):
        suffix = pre_b[2 * h : 2 * h + 2].reshape(ROWS, DV)
        gv_ref[:, cols[h]] = (gvacc[:, cols[h]] + tn(heavy(phik_sc[h]), suffix)).astype(BF)
        gk = gk + pull(kl, h, nt(suffix, v_ref[:, cols[h]]))
    gkl_ref[...] = gk.astype(BF)
    for copy in sends:
        copy.wait_send()


def shards(query_lin, key_lin, values, win_queries, win_keys, gain, grad_out):
    first, second = selectors()
    wide = jax.ShapeDtypeStruct((TOK, 2 * DV), BF)
    thin = jax.ShapeDtypeStruct((TOK, 2 * KD), BF)
    spec = pl.BlockSpec(memory_space=pltpu.VMEM)
    full = pltpu.VMEM((TOK, 2 * DV), BF)
    full32 = pltpu.VMEM((TOK, 2 * DV), F32)
    one = pltpu.VMEM((HALF, DV), BF)
    three = pltpu.VMEM((3, HALF, DV), BF)
    four = pltpu.VMEM((4, HALF, DV), BF)
    scan = [four, three, one, three, one, three, three, four]
    return pl.pallas_call(
        kernel,
        out_shape=(wide, thin, thin, wide, wide, wide),
        in_specs=[spec] * 9,
        out_specs=(spec,) * 6,
        scratch_shapes=[full] * 6
        + scan
        + scan
        + [
            pltpu.VMEM((8, TOK), F32),
            pltpu.VMEM((NH - 1, 8, TOK), F32),
            full32,
            full32,
            pltpu.VMEM((2, TOK, TOK), BF),
            full32,
            full32,
            pltpu.VMEM((2, ROWS, TOK), BF),
            pltpu.VMEM((2, ROWS, TOK), BF),
            pltpu.SemaphoreType.DMA((35,)),
            pltpu.SemaphoreType.DMA((35,)),
        ],
        compiler_params=pltpu.CompilerParams(collective_id=0, has_side_effects=True),
    )(
        query_lin, key_lin, values, win_queries, win_keys, gain.reshape(1, -1), grad_out,
        jnp.asarray(first, BF), jnp.asarray(second, BF),
    )


def solution(mesh):
    tiled = P("ctx", "head")
    return jax.shard_map(
        shards,
        mesh=mesh,
        in_specs=(tiled, tiled, tiled, tiled, tiled, P("head"), tiled),
        out_specs=(tiled,) * 6,
        check_vma=False,
    )
```

```python
import math

import jax
import jax.numpy as jnp
import numpy as np
from jax import lax
from jax.experimental import pallas as pl
from jax.experimental.pallas import tpu as pltpu
from jax.sharding import PartitionSpec as P

HEADS = 16
KD = 16
DV = 128
WD = 128
TOK = 128
GROUP = 16
GROUPS = 4
NH = 8
ROWS = 160
SLICE = 2 * ROWS // GROUP
PER = GROUP // 2
WIDTH = HEADS * DV
EPS = 1e-06
MESH = pl.DeviceIdType.MESH
BF = jnp.bfloat16
F32 = jnp.float32


def selectors():
    first = np.zeros((2 * ROWS, 2 * KD), np.float32)
    second = np.zeros((2 * ROWS, 2 * KD), np.float32)
    for h in range(2):
        base, lane = h * ROWS, h * KD
        for i in range(KD):
            first[base + 1 + i, lane + i] = 1
            first[base + 17 + i, lane + i] = 1
            second[base + 17 + i, lane + i] = 1
        row = base + 33
        for i in range(KD):
            for j in range(i + 1, KD):
                first[row, lane + i] = 1
                second[row, lane + j] = 1
                row += 1
    return first, second


def turned(table):
    return table.reshape(2, ROWS, 2 * KD).transpose(0, 2, 1)


def nn(a, b):
    return lax.dot_general(a, b, (((1,), (0,)), ((), ())), preferred_element_type=F32)


def nt(a, b):
    return lax.dot_general(a, b, (((1,), (1,)), ((), ())), preferred_element_type=F32)


def tn(a, b):
    return lax.dot_general(a, b, (((0,), (0,)), ((), ())), preferred_element_type=F32)


def kernel(
    ql_ref, kl_ref, v_ref, wq_ref, wk_ref, gain_ref, do_ref, e1_ref, e2_ref, f1_ref, f2_ref,
    mixed_ref, gql_ref, gkl_ref, gv_ref, gwq_ref, gwk_ref,
    krim, vrim, gkout, gvout, gkin, gvin,
    st_a, r1_a, t_a, rw_a, out_a, pre_a,
    st_b, r1_b, t_b, rw_b, out_b, pre_b,
    sums, sums_in, lin_sc, win_sc, ker_sc, gvacc, gkacc, phiq_sc, phik_sc,
    ss, rs,
):
    ctx = lax.axis_index("ctx")
    head = lax.axis_index("head")
    group = ctx // GROUP
    member = lax.rem(ctx, GROUP)
    sends = []

    def partner(d):
        return lax.rem(member + d, GROUP)

    def at(g, m):
        return {"ctx": lax.rem(g, GROUPS) * GROUP + lax.rem(m, GROUP)}

    count = GROUP * GROUPS
    ahead = {"ctx": lax.rem(ctx + 1, count)}
    behind = {"ctx": lax.rem(ctx + count - 1, count)}

    barrier = pltpu.get_barrier_semaphore()
    peers = [at(group, member + d) for d in range(1, GROUP)]
    peers += [at(group + j, member) for j in (1, 2, 3)]
    peers += [ahead, behind]
    peers += [{"head": lax.rem(head + d, NH)} for d in range(1, NH)]
    for peer in peers:
        pl.semaphore_signal(barrier, inc=1, device_id=peer, device_id_type=MESH)

    def send(src, dst, slot, device):
        copy = pltpu.make_async_remote_copy(
            src_ref=src, dst_ref=dst, send_sem=ss.at[slot], recv_sem=rs.at[slot],
            device_id=device, device_id_type=MESH,
        )
        copy.start()
        sends.append(copy)
        return copy

    def wait_all(copies):
        for copy in copies:
            copy.wait_recv()

    class Scan:
        def __init__(self, sign, base, st, r1, t, rw, out, pre):
            self.sign, self.base = sign, base
            self.st, self.r1, self.t, self.rw, self.out, self.pre = st, r1, t, rw, out, pre

        def start(self):
            self.c1 = [
                send(self.st.at[partner(d)], self.r1.at[member], self.base + d - 1, at(group, member + d))
                for d in range(1, GROUP)
            ]
            self.r1[member] = self.st[member]

        def groups(self):
            wait_all(self.c1)
            total = self.r1[0].astype(F32)
            for k in range(1, GROUP):
                total = total + self.r1[k].astype(F32)
            self.t[...] = total.astype(BF)
            self.c2 = [
                send(self.t, self.rw.at[j - 1], self.base + 14 + j, at(group + j, member))
                for j in (2, 1, 3)
            ]

        def spread(self):
            wait_all(self.c2)
            total = jnp.zeros((SLICE, DV), F32)
            for j in (1, 2, 3):
                source = lax.rem(group + GROUPS - j, GROUPS)
                earlier = source < group if self.sign > 0 else source > group
                total = total + self.rw[j - 1].astype(F32) * jnp.where(earlier, 1.0, 0.0).astype(F32)
            order = range(GROUP) if self.sign > 0 else range(GROUP - 1, -1, -1)
            for k in order:
                self.out[k] = total.astype(BF)
                total = total + self.r1[k].astype(F32)
            self.c3 = [
                send(self.out.at[partner(d)], self.pre.at[member], self.base + 17 + d, at(group, member + d))
                for d in range(1, GROUP)
            ]
            self.pre[member] = self.out[member]

        def finish(self):
            wait_all(self.c3)

        def state(self, h):
            rows = [self.pre[PER * h + k].astype(F32) for k in range(PER)]
            return jnp.concatenate(rows, axis=0).astype(BF)

        def put(self, h, state):
            for k in range(PER):
                self.st[PER * h + k] = state[k * SLICE : (k + 1) * SLICE].astype(BF)

    fwd = Scan(1, 0, st_a, r1_a, t_a, rw_a, out_a, pre_a)
    bwd = Scan(-1, 33, st_b, r1_b, t_b, rw_b, out_b, pre_b)

    row32 = lax.broadcasted_iota(jnp.int32, (2 * KD, TOK), 0)
    row = lax.broadcasted_iota(jnp.int32, (TOK, TOK), 0)
    col = lax.broadcasted_iota(jnp.int32, (TOK, TOK), 1)
    causal = col <= row
    frow = lax.broadcasted_iota(jnp.int32, (ROWS, TOK), 0)
    add_first = jnp.where(frow == 0, 1.0, 0.0)
    add_second = jnp.where(frow <= KD, 1.0, 0.0)
    pair_scale = 1.0 / (math.sqrt(2.0) * math.sqrt(KD))
    scale = jnp.where(frow == 0, 1.0, jnp.where(frow <= KD, 1.0 / math.sqrt(math.sqrt(KD)), pair_scale))
    weight = jnp.where(frow >= 33, 2.0, 1.0)

    def factors(x, h):
        rows = slice(h * ROWS, (h + 1) * ROWS)
        return nn(e1_ref[rows, :], x) + add_first, nn(e2_ref[rows, :], x) + add_second

    def phi(x, h):
        a, b = factors(x, h)
        return (a * b * scale).astype(BF)

    def heavy(features):
        return (features.astype(F32) * weight).astype(BF)

    def pull(x, h, cot):
        a, b = factors(x, h)
        cot = cot * (scale * weight)
        return nn(f1_ref[h], (cot * b).astype(BF)) + nn(f2_ref[h], (cot * a).astype(BF))

    def own(x, h):
        inside = (row32 >= h * KD) & (row32 < (h + 1) * KD)
        return jnp.where(inside, x.astype(F32), 0.0).astype(BF)

    cols = [slice(h * DV, (h + 1) * DV) for h in range(2)]
    ql, kl = ql_ref[...], kl_ref[...]

    for h in range(2):
        key_phi = phi(kl, h)
        phik_sc[h] = key_phi
        fwd.put(h, nn(key_phi, v_ref[:, cols[h]]))

    pl.semaphore_wait(barrier, len(peers))
    fwd.start()

    def lin_score(h):
        return tn(own(ql, h), kl) * (1.0 / math.sqrt(KD))

    for h in range(2):
        phiq_sc[h] = phi(ql, h)
        s = lin_score(h)
        ker = jnp.where(causal, 1.0 + s + 0.5 * s * s, 0.0).astype(BF)
        ker_sc[h] = ker
        lin_sc[:, cols[h]] = nn(ker, v_ref[:, cols[h]])

    fwd.groups()
    rim = [
        send(wk_ref, krim, 66, ahead),
        send(v_ref, vrim, 67, ahead),
    ]

    scale_win = 1.0 / math.sqrt(WD)
    edge = (col > row) & (ctx > 0)
    wait_all(rim)

    def window(h):
        c = cols[h]
        q, k1, k2 = wq_ref[:, c], krim[:, c], wk_ref[:, c]
        v1, v2, do = vrim[:, c], v_ref[:, c], do_ref[:, c]
        s1 = jnp.where(edge, nt(q, k1) * scale_win, -1e30)
        s2 = jnp.where(causal, nt(q, k2) * scale_win, -1e30)
        top = jnp.maximum(
            jnp.max(s1, axis=1, keepdims=True), jnp.max(s2, axis=1, keepdims=True)
        )
        x1 = jnp.where(edge, jnp.exp(s1 - top), 0.0)
        x2 = jnp.where(causal, jnp.exp(s2 - top), 0.0)
        inv = 1.0 / (jnp.sum(x1, axis=1, keepdims=True) + jnp.sum(x2, axis=1, keepdims=True))
        p1, p2 = x1 * inv, x2 * inv
        b1, b2 = p1.astype(BF), p2.astype(BF)
        out = nn(b1, v1) + nn(b2, v2)
        win_sc[:, c] = out
        delta = jnp.sum(do.astype(F32) * out, axis=1, keepdims=True)
        g1 = (p1 * (nt(do, v1) - delta)).astype(BF)
        g2 = (p2 * (nt(do, v2) - delta)).astype(BF)
        gkout[:, c] = (tn(g1, q) * scale_win).astype(BF)
        gvout[:, c] = tn(b1, do).astype(BF)
        gwq_ref[:, c] = ((nn(g1, k1) + nn(g2, k2)) * scale_win).astype(BF)
        gkacc[:, c] = tn(g2, q) * scale_win
        gvacc[:, c] = tn(b2, do)

    window(0)
    fwd.spread()
    window(1)
    back = [
        send(gkout, gkin, 68, behind),
        send(gvout, gvin, 69, behind),
    ]
    fwd.finish()

    gain = gain_ref[...]
    for h in range(2):
        prefix = fwd.state(h)
        lin_sc[:, cols[h]] += tn(heavy(phiq_sc[h]), prefix)
    lin = lin_sc[...]
    gd = gain * do_ref[...].astype(F32)
    square = jnp.sum(lin * lin, axis=1, keepdims=True)
    cross = jnp.sum(gd * lin, axis=1, keepdims=True)
    both = jnp.where(col == 0, square, jnp.where(col == 1, cross, 0.0))
    sums[...] = both.T[:8]
    shares = [
        send(sums, sums_in.at[d - 1], 69 + d, {"head": lax.rem(head + d, NH)})
        for d in range(1, NH)
    ]
    wait_all(shares)
    total = sums[...]
    for d in range(NH - 1):
        total = total + sums_in[d]
    total = jnp.concatenate([total, jnp.zeros((TOK - 8, TOK), F32)], axis=0).T
    square = jnp.sum(jnp.where(col == 0, total, 0.0), axis=1, keepdims=True)
    cross = jnp.sum(jnp.where(col == 1, total, 0.0), axis=1, keepdims=True)
    inverse = 1.0 / jnp.sqrt(square * (1.0 / WIDTH) + EPS)
    grad_lin = (
        inverse * gd - lin * (inverse * inverse * inverse * (cross * (1.0 / WIDTH)))
    ).astype(BF)
    for h in range(2):
        bwd.put(h, nn(phiq_sc[h], grad_lin[:, cols[h]]))
    bwd.start()
    mixed_ref[...] = (lin * inverse * gain + win_sc[...]).astype(BF)

    gq = jnp.zeros((2 * KD, TOK), F32)
    gk = jnp.zeros((2 * KD, TOK), F32)
    for h in range(2):
        gl = grad_lin[:, cols[h]]
        g = nt(gl, v_ref[:, cols[h]]) * (1.0 + lin_score(h))
        g = jnp.where(causal, g, 0.0).astype(BF)
        gq = gq + nt(own(kl, h), g) * (1.0 / math.sqrt(KD))
        gk = gk + nn(own(ql, h), g) * (1.0 / math.sqrt(KD))
    bwd.groups()
    for h in range(2):
        gl = grad_lin[:, cols[h]]
        prefix = fwd.state(h)
        gq = gq + pull(ql, h, nt(prefix, gl))
        gvacc[:, cols[h]] += tn(ker_sc[h], gl)
    gql_ref[...] = gq.astype(BF)
    bwd.spread()
    wait_all(back)
    gwk_ref[...] = (gkacc[...] + gkin[...].astype(F32)).astype(BF)
    gvacc[...] += gvin[...].astype(F32)
    bwd.finish()
    for h in range(2):
        suffix = bwd.state(h)
        gv_ref[:, cols[h]] = (gvacc[:, cols[h]] + tn(heavy(phik_sc[h]), suffix)).astype(BF)
        gk = gk + pull(kl, h, nt(suffix, v_ref[:, cols[h]]))
    gkl_ref[...] = gk.astype(BF)
    for copy in sends:
        copy.wait_send()


def shards(query_lin, key_lin, values, win_queries, win_keys, gain, grad_out):
    first, second = selectors()
    wide = jax.ShapeDtypeStruct((TOK, 2 * DV), BF)
    thin = jax.ShapeDtypeStruct((2 * KD, TOK), BF)
    spec = pl.BlockSpec(memory_space=pltpu.VMEM)
    full = pltpu.VMEM((TOK, 2 * DV), BF)
    full32 = pltpu.VMEM((TOK, 2 * DV), F32)
    one = pltpu.VMEM((SLICE, DV), BF)
    three = pltpu.VMEM((GROUPS - 1, SLICE, DV), BF)
    every = pltpu.VMEM((GROUP, SLICE, DV), BF)
    scan = [every, every, one, three, every, every]
    outs = pl.pallas_call(
        kernel,
        out_shape=(wide, thin, thin, wide, wide, wide),
        in_specs=[spec] * 11,
        out_specs=(spec,) * 6,
        scratch_shapes=[full] * 6
        + scan
        + scan
        + [
            pltpu.VMEM((8, TOK), F32),
            pltpu.VMEM((NH - 1, 8, TOK), F32),
            full32,
            full32,
            pltpu.VMEM((2, TOK, TOK), BF),
            full32,
            full32,
            pltpu.VMEM((2, ROWS, TOK), BF),
            pltpu.VMEM((2, ROWS, TOK), BF),
            pltpu.SemaphoreType.DMA((77,)),
            pltpu.SemaphoreType.DMA((77,)),
        ],
        compiler_params=pltpu.CompilerParams(collective_id=0, has_side_effects=True),
    )(
        query_lin.T, key_lin.T, values, win_queries, win_keys, gain.reshape(1, -1), grad_out,
        jnp.asarray(first, BF), jnp.asarray(second, BF),
        jnp.asarray(turned(first), BF), jnp.asarray(turned(second), BF),
    )
    return outs[0], outs[1].T, outs[2].T, outs[3], outs[4], outs[5]


def solution(mesh):
    tiled = P("ctx", "head")
    return jax.shard_map(
        shards,
        mesh=mesh,
        in_specs=(tiled, tiled, tiled, tiled, tiled, P("head"), tiled),
        out_specs=(tiled,) * 6,
        check_vma=False,
    )
```

```python
import math

import jax
import jax.numpy as jnp
import numpy as np
from jax import lax
from jax.experimental import pallas as pl
from jax.experimental.pallas import tpu as pltpu
from jax.sharding import PartitionSpec as P

HEADS = 16
KD = 16
DV = 128
WD = 128
TOK = 128
GROUP = 16
GROUPS = 4
NH = 8
ROWS = 160
SLICE = 2 * ROWS // GROUP
PER = GROUP // 2
WIDTH = HEADS * DV
EPS = 1e-06
MESH = pl.DeviceIdType.MESH
BF = jnp.bfloat16
F32 = jnp.float32


def selectors():
    first = np.zeros((2 * ROWS, 2 * KD), np.float32)
    second = np.zeros((2 * ROWS, 2 * KD), np.float32)
    for h in range(2):
        base, lane = h * ROWS, h * KD
        for i in range(KD):
            first[base + 1 + i, lane + i] = 1
            first[base + 17 + i, lane + i] = 1
            second[base + 17 + i, lane + i] = 1
        row = base + 33
        for i in range(KD):
            for j in range(i + 1, KD):
                first[row, lane + i] = 1
                second[row, lane + j] = 1
                row += 1
    return first, second


def turned(table):
    return table.reshape(2, ROWS, 2 * KD).transpose(0, 2, 1)


def nn(a, b):
    return lax.dot_general(a, b, (((1,), (0,)), ((), ())), preferred_element_type=F32)


def nt(a, b):
    return lax.dot_general(a, b, (((1,), (1,)), ((), ())), preferred_element_type=F32)


def tn(a, b):
    return lax.dot_general(a, b, (((0,), (0,)), ((), ())), preferred_element_type=F32)


def kernel(
    ql_in, kl_in, v_in, wq_in, wk_in, gain_in, do_in, e1_in, e2_in, f1_in, f2_in,
    mixed_ref, gql_ref, gkl_ref, gv_ref, gwq_ref, gwk_ref,
    krim, vrim, gkout, gvout, gkin, gvin,
    st_a, r1_a, t_a, rw_a, out_a, pre_a,
    st_b, r1_b, t_b, rw_b, out_b, pre_b,
    sums, sums_in, lin_sc, win_sc, ker_sc, gvacc, gkacc, phiq_sc, phik_sc,
    ss, rs,
    ql_ref, kl_ref, v_ref, wq_ref, wk_ref, gain_ref, do_ref, e1_ref, e2_ref, f1_ref, f2_ref,
    local, far,
):
    ctx = lax.axis_index("ctx")
    head = lax.axis_index("head")
    group = ctx // GROUP
    member = lax.rem(ctx, GROUP)
    sends = []

    def partner(d):
        return lax.rem(member + d, GROUP)

    def at(g, m):
        return {"ctx": lax.rem(g, GROUPS) * GROUP + lax.rem(m, GROUP)}

    count = GROUP * GROUPS
    ahead = {"ctx": lax.rem(ctx + 1, count)}
    behind = {"ctx": lax.rem(ctx + count - 1, count)}

    barrier = pltpu.get_barrier_semaphore()
    peers = [at(group, member + d) for d in range(1, GROUP)]
    peers += [at(group + j, member) for j in (1, 3)]
    peers += [ahead, behind]
    peers += [{"head": lax.rem(head + d, NH)} for d in range(1, NH)]
    for peer in peers:
        pl.semaphore_signal(barrier, inc=1, device_id=peer, device_id_type=MESH)

    inputs = (kl_in, e1_in, e2_in, v_in, ql_in, wk_in, wq_in, do_in, gain_in, f1_in, f2_in)
    held = (kl_ref, e1_ref, e2_ref, v_ref, ql_ref, wk_ref, wq_ref, do_ref, gain_ref, f1_ref, f2_ref)
    fetches = [
        pltpu.make_async_copy(source, target, local.at[i])
        for i, (source, target) in enumerate(zip(inputs, held))
    ]
    for fetch in fetches:
        fetch.start()
    for fetch in fetches:
        fetch.wait()

    def send(src, dst, slot, device):
        copy = pltpu.make_async_remote_copy(
            src_ref=src, dst_ref=dst, send_sem=ss.at[slot], recv_sem=rs.at[slot],
            device_id=device, device_id_type=MESH,
        )
        copy.start()
        sends.append(copy)
        return copy

    def wait_all(copies):
        for copy in copies:
            copy.wait_recv()

    class Scan:
        def __init__(self, sign, base, st, r1, t, rw, out, pre):
            self.sign, self.base = sign, base
            self.st, self.r1, self.t, self.rw, self.out, self.pre = st, r1, t, rw, out, pre

        def start(self):
            self.c1 = [
                send(self.st.at[partner(d)], self.r1.at[member], self.base + d - 1, at(group, member + d))
                for d in range(1, GROUP)
            ]
            self.r1[member] = self.st[member]

        def groups(self):
            wait_all(self.c1)
            total = self.r1[0].astype(F32)
            for k in range(1, GROUP):
                total = total + self.r1[k].astype(F32)
            self.t[...] = total.astype(BF)
            self.c2 = [
                send(self.t, self.rw.at[j - 1], self.base + 14 + j, at(group + j, member))
                for j in (2, 1, 3)
            ]

        def spread(self):
            wait_all(self.c2)
            total = jnp.zeros((SLICE, DV), F32)
            for j in (1, 2, 3):
                source = lax.rem(group + GROUPS - j, GROUPS)
                earlier = source < group if self.sign > 0 else source > group
                total = total + self.rw[j - 1].astype(F32) * jnp.where(earlier, 1.0, 0.0).astype(F32)
            order = range(GROUP) if self.sign > 0 else range(GROUP - 1, -1, -1)
            for k in order:
                self.out[k] = total.astype(BF)
                total = total + self.r1[k].astype(F32)
            self.c3 = [
                send(self.out.at[partner(d)], self.pre.at[member], self.base + 17 + d, at(group, member + d))
                for d in range(1, GROUP)
            ]
            self.pre[member] = self.out[member]

        def finish(self):
            wait_all(self.c3)

        def state(self, h):
            rows = [self.pre[PER * h + k].astype(F32) for k in range(PER)]
            return jnp.concatenate(rows, axis=0).astype(BF)

        def put(self, h, state):
            for k in range(PER):
                self.st[PER * h + k] = state[k * SLICE : (k + 1) * SLICE].astype(BF)

    fwd = Scan(1, 0, st_a, r1_a, t_a, rw_a, out_a, pre_a)
    bwd = Scan(-1, 33, st_b, r1_b, t_b, rw_b, out_b, pre_b)

    row32 = lax.broadcasted_iota(jnp.int32, (2 * KD, TOK), 0)
    row = lax.broadcasted_iota(jnp.int32, (TOK, TOK), 0)
    col = lax.broadcasted_iota(jnp.int32, (TOK, TOK), 1)
    causal = col <= row
    frow = lax.broadcasted_iota(jnp.int32, (ROWS, TOK), 0)
    add_first = jnp.where(frow == 0, 1.0, 0.0)
    add_second = jnp.where(frow <= KD, 1.0, 0.0)
    pair_scale = 1.0 / (math.sqrt(2.0) * math.sqrt(KD))
    scale = jnp.where(frow == 0, 1.0, jnp.where(frow <= KD, 1.0 / math.sqrt(math.sqrt(KD)), pair_scale))
    weight = jnp.where(frow >= 33, 2.0, 1.0)

    def factors(x, h):
        rows = slice(h * ROWS, (h + 1) * ROWS)
        return nn(e1_ref[rows, :], x) + add_first, nn(e2_ref[rows, :], x) + add_second

    def phi(x, h):
        a, b = factors(x, h)
        return (a * b * scale).astype(BF)

    def heavy(features):
        return (features.astype(F32) * weight).astype(BF)

    def pull(x, h, cot):
        a, b = factors(x, h)
        cot = cot * (scale * weight)
        return nn(f1_ref[h], (cot * b).astype(BF)) + nn(f2_ref[h], (cot * a).astype(BF))

    def own(x, h):
        inside = (row32 >= h * KD) & (row32 < (h + 1) * KD)
        return jnp.where(inside, x.astype(F32), 0.0).astype(BF)

    cols = [slice(h * DV, (h + 1) * DV) for h in range(2)]
    ql, kl = ql_ref[...], kl_ref[...]

    for h in range(2):
        key_phi = phi(kl, h)
        phik_sc[h] = key_phi
        fwd.put(h, nn(key_phi, v_ref[:, cols[h]]))

    pl.semaphore_wait(barrier, len(peers))
    pl.semaphore_signal(far, inc=1, device_id=at(group + 3, member), device_id_type=MESH)
    fwd.start()

    def lin_score(h):
        return tn(own(ql, h), kl) * (1.0 / math.sqrt(KD))

    for h in range(2):
        phiq_sc[h] = phi(ql, h)
        s = lin_score(h)
        ker = jnp.where(causal, 1.0 + s + 0.5 * s * s, 0.0).astype(BF)
        ker_sc[h] = ker
        lin_sc[:, cols[h]] = nn(ker, v_ref[:, cols[h]])

    pl.semaphore_wait(far, 1)
    fwd.groups()
    rim = [
        send(wk_ref, krim, 66, ahead),
        send(v_ref, vrim, 67, ahead),
    ]

    scale_win = 1.0 / math.sqrt(WD)
    edge = (col > row) & (ctx > 0)
    wait_all(rim)

    def window(h):
        c = cols[h]
        q, k1, k2 = wq_ref[:, c], krim[:, c], wk_ref[:, c]
        v1, v2, do = vrim[:, c], v_ref[:, c], do_ref[:, c]
        s1 = jnp.where(edge, nt(q, k1) * scale_win, -1e30)
        s2 = jnp.where(causal, nt(q, k2) * scale_win, -1e30)
        top = jnp.maximum(
            jnp.max(s1, axis=1, keepdims=True), jnp.max(s2, axis=1, keepdims=True)
        )
        x1 = jnp.where(edge, jnp.exp(s1 - top), 0.0)
        x2 = jnp.where(causal, jnp.exp(s2 - top), 0.0)
        inv = 1.0 / (jnp.sum(x1, axis=1, keepdims=True) + jnp.sum(x2, axis=1, keepdims=True))
        p1, p2 = x1 * inv, x2 * inv
        b1, b2 = p1.astype(BF), p2.astype(BF)
        out = nn(b1, v1) + nn(b2, v2)
        win_sc[:, c] = out
        delta = jnp.sum(do.astype(F32) * out, axis=1, keepdims=True)
        g1 = (p1 * (nt(do, v1) - delta)).astype(BF)
        g2 = (p2 * (nt(do, v2) - delta)).astype(BF)
        gkout[:, c] = (tn(g1, q) * scale_win).astype(BF)
        gvout[:, c] = tn(b1, do).astype(BF)
        gwq_ref[:, c] = ((nn(g1, k1) + nn(g2, k2)) * scale_win).astype(BF)
        gkacc[:, c] = tn(g2, q) * scale_win
        gvacc[:, c] = tn(b2, do)

    window(0)
    fwd.spread()
    window(1)
    back = [
        send(gkout, gkin, 68, behind),
        send(gvout, gvin, 69, behind),
    ]
    fwd.finish()

    gain = gain_ref[...]
    for h in range(2):
        prefix = fwd.state(h)
        lin_sc[:, cols[h]] += tn(heavy(phiq_sc[h]), prefix)
    lin = lin_sc[...]
    gd = gain * do_ref[...].astype(F32)
    square = jnp.sum(lin * lin, axis=1, keepdims=True)
    cross = jnp.sum(gd * lin, axis=1, keepdims=True)
    both = jnp.where(col == 0, square, jnp.where(col == 1, cross, 0.0))
    sums[...] = both.T[:8]
    shares = [
        send(sums, sums_in.at[d - 1], 69 + d, {"head": lax.rem(head + d, NH)})
        for d in range(1, NH)
    ]
    wait_all(shares)
    total = sums[...]
    for d in range(NH - 1):
        total = total + sums_in[d]
    total = jnp.concatenate([total, jnp.zeros((TOK - 8, TOK), F32)], axis=0).T
    square = jnp.sum(jnp.where(col == 0, total, 0.0), axis=1, keepdims=True)
    cross = jnp.sum(jnp.where(col == 1, total, 0.0), axis=1, keepdims=True)
    inverse = 1.0 / jnp.sqrt(square * (1.0 / WIDTH) + EPS)
    grad_lin = (
        inverse * gd - lin * (inverse * inverse * inverse * (cross * (1.0 / WIDTH)))
    ).astype(BF)
    for h in range(2):
        bwd.put(h, nn(phiq_sc[h], grad_lin[:, cols[h]]))
    bwd.start()
    mixed_ref[...] = (lin * inverse * gain + win_sc[...]).astype(BF)

    gq = jnp.zeros((2 * KD, TOK), F32)
    gk = jnp.zeros((2 * KD, TOK), F32)
    for h in range(2):
        gl = grad_lin[:, cols[h]]
        g = nt(gl, v_ref[:, cols[h]]) * (1.0 + lin_score(h))
        g = jnp.where(causal, g, 0.0).astype(BF)
        gq = gq + nt(own(kl, h), g) * (1.0 / math.sqrt(KD))
        gk = gk + nn(own(ql, h), g) * (1.0 / math.sqrt(KD))
    bwd.groups()
    for h in range(2):
        gl = grad_lin[:, cols[h]]
        prefix = fwd.state(h)
        gq = gq + pull(ql, h, nt(prefix, gl))
        gvacc[:, cols[h]] += tn(ker_sc[h], gl)
    gql_ref[...] = gq.astype(BF)
    bwd.spread()
    wait_all(back)
    gwk_ref[...] = (gkacc[...] + gkin[...].astype(F32)).astype(BF)
    gvacc[...] += gvin[...].astype(F32)
    bwd.finish()
    for h in range(2):
        suffix = bwd.state(h)
        gv_ref[:, cols[h]] = (gvacc[:, cols[h]] + tn(heavy(phik_sc[h]), suffix)).astype(BF)
        gk = gk + pull(kl, h, nt(suffix, v_ref[:, cols[h]]))
    gkl_ref[...] = gk.astype(BF)
    for copy in sends:
        copy.wait_send()


def shards(query_lin, key_lin, values, win_queries, win_keys, gain, grad_out):
    first, second = selectors()
    wide = jax.ShapeDtypeStruct((TOK, 2 * DV), BF)
    thin = jax.ShapeDtypeStruct((2 * KD, TOK), BF)
    spec = pl.BlockSpec(memory_space=pltpu.VMEM)
    full = pltpu.VMEM((TOK, 2 * DV), BF)
    full32 = pltpu.VMEM((TOK, 2 * DV), F32)
    one = pltpu.VMEM((SLICE, DV), BF)
    three = pltpu.VMEM((GROUPS - 1, SLICE, DV), BF)
    every = pltpu.VMEM((GROUP, SLICE, DV), BF)
    scan = [every, every, one, three, every, every]
    outs = pl.pallas_call(
        kernel,
        out_shape=(wide, thin, thin, wide, wide, wide),
        in_specs=[pl.BlockSpec(memory_space=pl.ANY)] * 11,
        out_specs=(spec,) * 6,
        scratch_shapes=[full] * 6
        + scan
        + scan
        + [
            pltpu.VMEM((8, TOK), F32),
            pltpu.VMEM((NH - 1, 8, TOK), F32),
            full32,
            full32,
            pltpu.VMEM((2, TOK, TOK), BF),
            full32,
            full32,
            pltpu.VMEM((2, ROWS, TOK), BF),
            pltpu.VMEM((2, ROWS, TOK), BF),
            pltpu.SemaphoreType.DMA((77,)),
            pltpu.SemaphoreType.DMA((77,)),
            pltpu.VMEM((2 * KD, TOK), BF),
            pltpu.VMEM((2 * KD, TOK), BF),
            full,
            full,
            full,
            pltpu.VMEM((1, 2 * DV), F32),
            full,
            pltpu.VMEM((2 * ROWS, 2 * KD), BF),
            pltpu.VMEM((2 * ROWS, 2 * KD), BF),
            pltpu.VMEM((2, 2 * KD, ROWS), BF),
            pltpu.VMEM((2, 2 * KD, ROWS), BF),
            pltpu.SemaphoreType.DMA((11,)),
            pltpu.SemaphoreType.REGULAR,
        ],
        compiler_params=pltpu.CompilerParams(collective_id=0, has_side_effects=True),
    )(
        query_lin.T, key_lin.T, values, win_queries, win_keys, gain.reshape(1, -1), grad_out,
        jnp.asarray(first, BF), jnp.asarray(second, BF),
        jnp.asarray(turned(first), BF), jnp.asarray(turned(second), BF),
    )
    def forward(*refs):
        for source, target in zip(refs[:6], refs[6:]):
            target[...] = source[...]

    outs = pl.pallas_call(
        forward,
        out_shape=(wide, thin, thin, wide, wide, wide),
        in_specs=[spec] * 6,
        out_specs=(spec,) * 6,
    )(*outs)
    return outs[0], outs[1].T, outs[2].T, outs[3], outs[4], outs[5]


def solution(mesh):
    tiled = P("ctx", "head")
    return jax.shard_map(
        shards,
        mesh=mesh,
        in_specs=(tiled, tiled, tiled, tiled, tiled, P("head"), tiled),
        out_specs=(tiled,) * 6,
        check_vma=False,
    )
```

```python
import math

import jax
import jax.numpy as jnp
import numpy as np
from jax import lax
from jax.experimental import pallas as pl
from jax.experimental.pallas import tpu as pltpu
from jax.sharding import PartitionSpec as P

HEADS = 16
KD = 16
DV = 128
WD = 128
TOK = 128
GROUP = 8
GROUPS = 8
FAR_FIRST = (4, 3, 5, 2, 6, 1, 7)
ROUND = (2, 6, 3, 5, 1, 7, 4)
NH = 8
ROWS = 160
SLICE = 2 * ROWS // GROUP
PER = GROUP // 2
WIDTH = HEADS * DV
EPS = 1e-06
MESH = pl.DeviceIdType.MESH
BF = jnp.bfloat16
F32 = jnp.float32


def selectors():
    first = np.zeros((2 * ROWS, 2 * KD), np.float32)
    second = np.zeros((2 * ROWS, 2 * KD), np.float32)
    for h in range(2):
        base, lane = h * ROWS, h * KD
        for i in range(KD):
            first[base + 1 + i, lane + i] = 1
            first[base + 17 + i, lane + i] = 1
            second[base + 17 + i, lane + i] = 1
        row = base + 33
        for i in range(KD):
            for j in range(i + 1, KD):
                first[row, lane + i] = 1
                second[row, lane + j] = 1
                row += 1
    return first, second


def turned(table):
    return table.reshape(2, ROWS, 2 * KD).transpose(0, 2, 1)


def nn(a, b):
    return lax.dot_general(a, b, (((1,), (0,)), ((), ())), preferred_element_type=F32)


def nt(a, b):
    return lax.dot_general(a, b, (((1,), (1,)), ((), ())), preferred_element_type=F32)


def tn(a, b):
    return lax.dot_general(a, b, (((0,), (0,)), ((), ())), preferred_element_type=F32)


def kernel(
    ql_in, kl_in, v_in, wq_in, wk_in, gain_in, do_in, e1_in, e2_in, f1_in, f2_in,
    mixed_ref, gql_ref, gkl_ref, gv_ref, gwq_ref, gwk_ref,
    krim, vrim, gkout, gvout, gkin, gvin,
    st_a, r1_a, t_a, rw_a, out_a, pre_a,
    st_b, r1_b, t_b, rw_b, out_b, pre_b,
    sums, sums_in, lin_sc, win_sc, ker_sc, gvacc, gkacc, phiq_sc, phik_sc,
    ss, rs,
    ql_ref, kl_ref, v_ref, wq_ref, wk_ref, gain_ref, do_ref, e1_ref, e2_ref, f1_ref, f2_ref,
    local, far,
):
    ctx = lax.axis_index("ctx")
    head = lax.axis_index("head")
    group = ctx // GROUP
    member = lax.rem(ctx, GROUP)
    sends = []

    def partner(d):
        return lax.rem(member + d, GROUP)

    def at(g, m):
        return {"ctx": lax.rem(g, GROUPS) * GROUP + lax.rem(m, GROUP)}

    count = GROUP * GROUPS
    ahead = {"ctx": lax.rem(ctx + 1, count)}
    behind = {"ctx": lax.rem(ctx + count - 1, count)}

    rw_a[...] = jnp.zeros_like(rw_a)
    rw_b[...] = jnp.zeros_like(rw_b)

    barrier = pltpu.get_barrier_semaphore()
    peers = [at(group + j, member) for j in (2, 6)]
    peers += [at(group, member + d) for d in ROUND]
    peers += [at(group + j, member) for j in (1, 7)]
    peers += [ahead, behind]
    peers += [{"head": lax.rem(head + d, NH)} for d in range(1, NH)]
    for peer in peers:
        pl.semaphore_signal(barrier, inc=1, device_id=peer, device_id_type=MESH)

    inputs = (kl_in, e1_in, e2_in, v_in, ql_in, wk_in, wq_in, do_in, gain_in, f1_in, f2_in)
    held = (kl_ref, e1_ref, e2_ref, v_ref, ql_ref, wk_ref, wq_ref, do_ref, gain_ref, f1_ref, f2_ref)
    fetches = [
        pltpu.make_async_copy(source, target, local.at[i])
        for i, (source, target) in enumerate(zip(inputs, held))
    ]
    for fetch in fetches:
        fetch.start()
    for fetch in fetches:
        fetch.wait()

    def send(src, dst, slot, device):
        copy = pltpu.make_async_remote_copy(
            src_ref=src, dst_ref=dst, send_sem=ss.at[slot], recv_sem=rs.at[slot],
            device_id=device, device_id_type=MESH,
        )
        copy.start()
        sends.append(copy)
        return copy

    def wait_all(copies):
        for copy in copies:
            copy.wait_recv()

    class Scan:
        def __init__(self, sign, base, st, r1, t, rw, out, pre):
            self.sign, self.base = sign, base
            self.st, self.r1, self.t, self.rw, self.out, self.pre = st, r1, t, rw, out, pre

        def start(self):
            self.c1 = [
                send(self.st.at[partner(d)], self.r1.at[member], self.base + d - 1, at(group, member + d))
                for d in ROUND
            ]
            self.r1[member] = self.st[member]

        def groups(self):
            wait_all(self.c1)
            total = self.r1[0].astype(F32)
            for k in range(1, GROUP):
                total = total + self.r1[k].astype(F32)
            self.t[...] = total.astype(BF)
            self.c2 = []
            for j in FAR_FIRST:
                copy = pltpu.make_async_remote_copy(
                    src_ref=self.t, dst_ref=self.rw.at[j - 1],
                    send_sem=ss.at[self.base + 6 + j], recv_sem=rs.at[self.base + 6 + j],
                    device_id=at(group + j, member), device_id_type=MESH,
                )
                up = group + j < GROUPS
                sent = up if self.sign > 0 else group + j >= GROUPS
                got = group >= j if self.sign > 0 else group < j
                pl.when(sent)(copy.start)
                self.c2.append((copy, sent, got))

        def spread(self):
            for copy, _, got in self.c2:
                pl.when(got)(copy.wait_recv)
            total = self.rw[0].astype(F32)
            for j in range(1, GROUPS - 1):
                total = total + self.rw[j].astype(F32)
            order = range(GROUP) if self.sign > 0 else range(GROUP - 1, -1, -1)
            for k in order:
                self.out[k] = total.astype(BF)
                total = total + self.r1[k].astype(F32)
            self.c3 = [
                send(self.out.at[partner(d)], self.pre.at[member], self.base + 13 + d, at(group, member + d))
                for d in ROUND
            ]
            self.pre[member] = self.out[member]

        def finish(self):
            wait_all(self.c3)

        def state(self, h):
            rows = [self.pre[PER * h + k].astype(F32) for k in range(PER)]
            return jnp.concatenate(rows, axis=0).astype(BF)

        def put(self, h, state):
            for k in range(PER):
                self.st[PER * h + k] = state[k * SLICE : (k + 1) * SLICE].astype(BF)

    fwd = Scan(1, 0, st_a, r1_a, t_a, rw_a, out_a, pre_a)
    bwd = Scan(-1, 21, st_b, r1_b, t_b, rw_b, out_b, pre_b)

    row32 = lax.broadcasted_iota(jnp.int32, (2 * KD, TOK), 0)
    row = lax.broadcasted_iota(jnp.int32, (TOK, TOK), 0)
    col = lax.broadcasted_iota(jnp.int32, (TOK, TOK), 1)
    causal = col <= row
    frow = lax.broadcasted_iota(jnp.int32, (ROWS, TOK), 0)
    add_first = jnp.where(frow == 0, 1.0, 0.0)
    add_second = jnp.where(frow <= KD, 1.0, 0.0)
    pair_scale = 1.0 / (math.sqrt(2.0) * math.sqrt(KD))
    scale = jnp.where(frow == 0, 1.0, jnp.where(frow <= KD, 1.0 / math.sqrt(math.sqrt(KD)), pair_scale))
    weight = jnp.where(frow >= 33, 2.0, 1.0)

    def factors(x, h):
        rows = slice(h * ROWS, (h + 1) * ROWS)
        return nn(e1_ref[rows, :], x) + add_first, nn(e2_ref[rows, :], x) + add_second

    def phi(x, h):
        a, b = factors(x, h)
        return (a * b * scale).astype(BF)

    def heavy(features):
        return (features.astype(F32) * weight).astype(BF)

    def pull(x, h, cot):
        a, b = factors(x, h)
        cot = cot * (scale * weight)
        return nn(f1_ref[h], (cot * b).astype(BF)) + nn(f2_ref[h], (cot * a).astype(BF))

    def own(x, h):
        inside = (row32 >= h * KD) & (row32 < (h + 1) * KD)
        return jnp.where(inside, x.astype(F32), 0.0).astype(BF)

    cols = [slice(h * DV, (h + 1) * DV) for h in range(2)]
    ql, kl = ql_ref[...], kl_ref[...]

    for h in range(2):
        key_phi = phi(kl, h)
        phik_sc[h] = key_phi
        fwd.put(h, nn(key_phi, v_ref[:, cols[h]]))

    pl.semaphore_wait(barrier, len(peers))
    for j in (2, 6):
        pl.semaphore_signal(far, inc=1, device_id=at(group + j, member), device_id_type=MESH)
    fwd.start()

    def lin_score(h):
        return tn(own(ql, h), kl) * (1.0 / math.sqrt(KD))

    for h in range(2):
        phiq_sc[h] = phi(ql, h)
        s = lin_score(h)
        ker = jnp.where(causal, 1.0 + s + 0.5 * s * s, 0.0).astype(BF)
        ker_sc[h] = ker
        lin_sc[:, cols[h]] = nn(ker, v_ref[:, cols[h]])

    pl.semaphore_wait(far, 2)
    fwd.groups()
    rim = [
        send(wk_ref, krim, 42, ahead),
        send(v_ref, vrim, 43, ahead),
    ]

    scale_win = 1.0 / math.sqrt(WD)
    edge = (col > row) & (ctx > 0)
    wait_all(rim)

    def window(h):
        c = cols[h]
        q, k1, k2 = wq_ref[:, c], krim[:, c], wk_ref[:, c]
        v1, v2, do = vrim[:, c], v_ref[:, c], do_ref[:, c]
        s1 = jnp.where(edge, nt(q, k1) * scale_win, -1e30)
        s2 = jnp.where(causal, nt(q, k2) * scale_win, -1e30)
        top = jnp.maximum(
            jnp.max(s1, axis=1, keepdims=True), jnp.max(s2, axis=1, keepdims=True)
        )
        x1 = jnp.where(edge, jnp.exp(s1 - top), 0.0)
        x2 = jnp.where(causal, jnp.exp(s2 - top), 0.0)
        inv = 1.0 / (jnp.sum(x1, axis=1, keepdims=True) + jnp.sum(x2, axis=1, keepdims=True))
        p1, p2 = x1 * inv, x2 * inv
        b1, b2 = p1.astype(BF), p2.astype(BF)
        out = nn(b1, v1) + nn(b2, v2)
        win_sc[:, c] = out
        delta = jnp.sum(do.astype(F32) * out, axis=1, keepdims=True)
        g1 = (p1 * (nt(do, v1) - delta)).astype(BF)
        g2 = (p2 * (nt(do, v2) - delta)).astype(BF)
        gkout[:, c] = (tn(g1, q) * scale_win).astype(BF)
        gvout[:, c] = tn(b1, do).astype(BF)
        gwq_ref[:, c] = ((nn(g1, k1) + nn(g2, k2)) * scale_win).astype(BF)
        gkacc[:, c] = tn(g2, q) * scale_win
        gvacc[:, c] = tn(b2, do)

    window(0)
    fwd.spread()
    window(1)
    fwd.finish()

    gain = gain_ref[...]
    for h in range(2):
        prefix = fwd.state(h)
        lin_sc[:, cols[h]] += tn(heavy(phiq_sc[h]), prefix)
    lin = lin_sc[...]
    gd = gain * do_ref[...].astype(F32)
    square = jnp.sum(lin * lin, axis=1, keepdims=True)
    cross = jnp.sum(gd * lin, axis=1, keepdims=True)
    both = jnp.where(col == 0, square, jnp.where(col == 1, cross, 0.0))
    sums[...] = both.T[:8]
    shares = [
        send(sums, sums_in.at[d - 1], 45 + d, {"head": lax.rem(head + d, NH)})
        for d in range(1, NH)
    ]
    back = [
        send(gkout, gkin, 44, behind),
        send(gvout, gvin, 45, behind),
    ]
    wait_all(shares)
    total = sums[...]
    for d in range(NH - 1):
        total = total + sums_in[d]
    total = jnp.concatenate([total, jnp.zeros((TOK - 8, TOK), F32)], axis=0).T
    square = jnp.sum(jnp.where(col == 0, total, 0.0), axis=1, keepdims=True)
    cross = jnp.sum(jnp.where(col == 1, total, 0.0), axis=1, keepdims=True)
    inverse = 1.0 / jnp.sqrt(square * (1.0 / WIDTH) + EPS)
    grad_lin = (
        inverse * gd - lin * (inverse * inverse * inverse * (cross * (1.0 / WIDTH)))
    ).astype(BF)
    for h in range(2):
        bwd.put(h, nn(phiq_sc[h], grad_lin[:, cols[h]]))
    bwd.start()
    mixed_ref[...] = (lin * inverse * gain + win_sc[...]).astype(BF)

    gq = jnp.zeros((2 * KD, TOK), F32)
    gk = jnp.zeros((2 * KD, TOK), F32)
    for h in range(2):
        gl = grad_lin[:, cols[h]]
        g = nt(gl, v_ref[:, cols[h]]) * (1.0 + lin_score(h))
        g = jnp.where(causal, g, 0.0).astype(BF)
        gq = gq + nt(own(kl, h), g) * (1.0 / math.sqrt(KD))
        gk = gk + nn(own(ql, h), g) * (1.0 / math.sqrt(KD))
    bwd.groups()
    for h in range(2):
        gl = grad_lin[:, cols[h]]
        prefix = fwd.state(h)
        gq = gq + pull(ql, h, nt(prefix, gl))
        gvacc[:, cols[h]] += tn(ker_sc[h], gl)
    gql_ref[...] = gq.astype(BF)
    bwd.spread()
    wait_all(back)
    gwk_ref[...] = (gkacc[...] + gkin[...].astype(F32)).astype(BF)
    gvacc[...] += gvin[...].astype(F32)
    bwd.finish()
    for h in range(2):
        suffix = bwd.state(h)
        gv_ref[:, cols[h]] = (gvacc[:, cols[h]] + tn(heavy(phik_sc[h]), suffix)).astype(BF)
        gk = gk + pull(kl, h, nt(suffix, v_ref[:, cols[h]]))
    gkl_ref[...] = gk.astype(BF)
    for copy in sends:
        copy.wait_send()
    for copy, sent, _ in fwd.c2 + bwd.c2:
        pl.when(sent)(copy.wait_send)


def shards(query_lin, key_lin, values, win_queries, win_keys, gain, grad_out):
    first, second = selectors()
    wide = jax.ShapeDtypeStruct((TOK, 2 * DV), BF)
    thin = jax.ShapeDtypeStruct((2 * KD, TOK), BF)
    spec = pl.BlockSpec(memory_space=pltpu.VMEM)
    full = pltpu.VMEM((TOK, 2 * DV), BF)
    full32 = pltpu.VMEM((TOK, 2 * DV), F32)
    one = pltpu.VMEM((SLICE, DV), BF)
    three = pltpu.VMEM((GROUPS - 1, SLICE, DV), BF)
    every = pltpu.VMEM((GROUP, SLICE, DV), BF)
    scan = [every, every, one, three, every, every]
    outs = pl.pallas_call(
        kernel,
        out_shape=(wide, thin, thin, wide, wide, wide),
        in_specs=[pl.BlockSpec(memory_space=pl.ANY)] * 11,
        out_specs=(spec,) * 6,
        scratch_shapes=[full] * 6
        + scan
        + scan
        + [
            pltpu.VMEM((8, TOK), F32),
            pltpu.VMEM((NH - 1, 8, TOK), F32),
            full32,
            full32,
            pltpu.VMEM((2, TOK, TOK), BF),
            full32,
            full32,
            pltpu.VMEM((2, ROWS, TOK), BF),
            pltpu.VMEM((2, ROWS, TOK), BF),
            pltpu.SemaphoreType.DMA((53,)),
            pltpu.SemaphoreType.DMA((53,)),
            pltpu.VMEM((2 * KD, TOK), BF),
            pltpu.VMEM((2 * KD, TOK), BF),
            full,
            full,
            full,
            pltpu.VMEM((1, 2 * DV), F32),
            full,
            pltpu.VMEM((2 * ROWS, 2 * KD), BF),
            pltpu.VMEM((2 * ROWS, 2 * KD), BF),
            pltpu.VMEM((2, 2 * KD, ROWS), BF),
            pltpu.VMEM((2, 2 * KD, ROWS), BF),
            pltpu.SemaphoreType.DMA((11,)),
            pltpu.SemaphoreType.REGULAR,
        ],
        compiler_params=pltpu.CompilerParams(collective_id=0, has_side_effects=True),
    )(
        query_lin.T, key_lin.T, values, win_queries, win_keys, gain.reshape(1, -1), grad_out,
        jnp.asarray(first, BF), jnp.asarray(second, BF),
        jnp.asarray(turned(first), BF), jnp.asarray(turned(second), BF),
    )
    def forward(*refs):
        for source, target in zip(refs[:6], refs[6:]):
            target[...] = source[...]

    outs = pl.pallas_call(
        forward,
        out_shape=(wide, thin, thin, wide, wide, wide),
        in_specs=[spec] * 6,
        out_specs=(spec,) * 6,
    )(*outs)
    return outs[0], outs[1].T, outs[2].T, outs[3], outs[4], outs[5]


def solution(mesh):
    tiled = P("ctx", "head")
    return jax.shard_map(
        shards,
        mesh=mesh,
        in_specs=(tiled, tiled, tiled, tiled, tiled, P("head"), tiled),
        out_specs=(tiled,) * 6,
        check_vma=False,
    )
```

```python
import math

import jax
import jax.numpy as jnp
import numpy as np
from jax import lax
from jax.experimental import pallas as pl
from jax.experimental.pallas import tpu as pltpu
from jax.sharding import PartitionSpec as P

HEADS = 16
KD = 16
DV = 128
WD = 128
TOK = 128
GROUP = 8
GROUPS = 8
FAR_FIRST = (4, 3, 5, 2, 6, 1, 7)
ROUND = (2, 6, 3, 5, 1, 7, 4)
NH = 8
ROWS = 160
SLICE = 2 * ROWS // GROUP
PER = GROUP // 2
WIDTH = HEADS * DV
EPS = 1e-06
MESH = pl.DeviceIdType.MESH
BF = jnp.bfloat16
F32 = jnp.float32


def selectors():
    first = np.zeros((2 * ROWS, 2 * KD), np.float32)
    second = np.zeros((2 * ROWS, 2 * KD), np.float32)
    for h in range(2):
        base, lane = h * ROWS, h * KD
        for i in range(KD):
            first[base + 1 + i, lane + i] = 1
            first[base + 17 + i, lane + i] = 1
            second[base + 17 + i, lane + i] = 1
        row = base + 33
        for i in range(KD):
            for j in range(i + 1, KD):
                first[row, lane + i] = 1
                second[row, lane + j] = 1
                row += 1
    return first, second


def turned(table):
    return table.reshape(2, ROWS, 2 * KD).transpose(0, 2, 1)


def nn(a, b):
    return lax.dot_general(a, b, (((1,), (0,)), ((), ())), preferred_element_type=F32)


def nt(a, b):
    return lax.dot_general(a, b, (((1,), (1,)), ((), ())), preferred_element_type=F32)


def tn(a, b):
    return lax.dot_general(a, b, (((0,), (0,)), ((), ())), preferred_element_type=F32)


def kernel(
    ql_in, kl_in, v_in, wq_in, wk_in, gain_in, do_in, e1_in, e2_in, f1_in, f2_in,
    mixed_out, gql_out, gkl_out, gv_out, gwq_out, gwk_out,
    krim, vrim, gkout, gvout, gkin, gvin,
    st_a, r1_a, t_a, rw_a, out_a, pre_a,
    st_b, r1_b, t_b, rw_b, out_b, pre_b,
    sums, sums_in, lin_sc, win_sc, ker_sc, gvacc, gkacc, phiq_sc, phik_sc,
    ss, rs,
    ql_ref, kl_ref, v_ref, wq_ref, wk_ref, gain_ref, do_ref, e1_ref, e2_ref, f1_ref, f2_ref,
    local, far, leave, mixed_ref, gql_ref, gkl_ref, gv_ref, gwq_ref, gwk_ref,
):
    ctx = lax.axis_index("ctx")
    head = lax.axis_index("head")
    group = ctx // GROUP
    member = lax.rem(ctx, GROUP)
    sends = []

    def partner(d):
        return lax.rem(member + d, GROUP)

    def at(g, m):
        return {"ctx": lax.rem(g, GROUPS) * GROUP + lax.rem(m, GROUP)}

    count = GROUP * GROUPS
    ahead = {"ctx": lax.rem(ctx + 1, count)}
    behind = {"ctx": lax.rem(ctx + count - 1, count)}

    rw_a[...] = jnp.zeros_like(rw_a)
    rw_b[...] = jnp.zeros_like(rw_b)

    barrier = pltpu.get_barrier_semaphore()
    peers = [at(group + j, member) for j in (2, 6)]
    peers += [at(group, member + d) for d in ROUND]
    peers += [at(group + j, member) for j in (1, 7)]
    peers += [ahead, behind]
    peers += [{"head": lax.rem(head + d, NH)} for d in range(1, NH)]
    for peer in peers:
        pl.semaphore_signal(barrier, inc=1, device_id=peer, device_id_type=MESH)

    inputs = (kl_in, e1_in, e2_in, v_in, ql_in, wk_in, wq_in, do_in, gain_in, f1_in, f2_in)
    held = (kl_ref, e1_ref, e2_ref, v_ref, ql_ref, wk_ref, wq_ref, do_ref, gain_ref, f1_ref, f2_ref)
    fetches = [
        pltpu.make_async_copy(source, target, local.at[i])
        for i, (source, target) in enumerate(zip(inputs, held))
    ]
    for fetch in fetches:
        fetch.start()
    for fetch in fetches:
        fetch.wait()

    def send(src, dst, slot, device):
        copy = pltpu.make_async_remote_copy(
            src_ref=src, dst_ref=dst, send_sem=ss.at[slot], recv_sem=rs.at[slot],
            device_id=device, device_id_type=MESH,
        )
        copy.start()
        sends.append(copy)
        return copy

    def wait_all(copies):
        for copy in copies:
            copy.wait_recv()

    class Scan:
        def __init__(self, sign, base, st, r1, t, rw, out, pre):
            self.sign, self.base = sign, base
            self.st, self.r1, self.t, self.rw, self.out, self.pre = st, r1, t, rw, out, pre

        def start(self):
            self.c1 = [
                send(self.st.at[partner(d)], self.r1.at[member], self.base + d - 1, at(group, member + d))
                for d in ROUND
            ]
            self.r1[member] = self.st[member]

        def groups(self):
            wait_all(self.c1)
            total = self.r1[0].astype(F32)
            for k in range(1, GROUP):
                total = total + self.r1[k].astype(F32)
            self.t[...] = total.astype(BF)
            self.c2 = []
            for j in FAR_FIRST:
                copy = pltpu.make_async_remote_copy(
                    src_ref=self.t, dst_ref=self.rw.at[j - 1],
                    send_sem=ss.at[self.base + 6 + j], recv_sem=rs.at[self.base + 6 + j],
                    device_id=at(group + j, member), device_id_type=MESH,
                )
                up = group + j < GROUPS
                sent = up if self.sign > 0 else group + j >= GROUPS
                got = group >= j if self.sign > 0 else group < j
                pl.when(sent)(copy.start)
                self.c2.append((copy, sent, got))

        def spread(self):
            for copy, _, got in self.c2:
                pl.when(got)(copy.wait_recv)
            total = self.rw[0].astype(F32)
            for j in range(1, GROUPS - 1):
                total = total + self.rw[j].astype(F32)
            order = range(GROUP) if self.sign > 0 else range(GROUP - 1, -1, -1)
            for k in order:
                self.out[k] = total.astype(BF)
                total = total + self.r1[k].astype(F32)
            self.c3 = [
                send(self.out.at[partner(d)], self.pre.at[member], self.base + 13 + d, at(group, member + d))
                for d in ROUND
            ]
            self.pre[member] = self.out[member]

        def finish(self):
            wait_all(self.c3)

        def state(self, h):
            rows = [self.pre[PER * h + k].astype(F32) for k in range(PER)]
            return jnp.concatenate(rows, axis=0).astype(BF)

        def put(self, h, state):
            for k in range(PER):
                self.st[PER * h + k] = state[k * SLICE : (k + 1) * SLICE].astype(BF)

    fwd = Scan(1, 0, st_a, r1_a, t_a, rw_a, out_a, pre_a)
    bwd = Scan(-1, 21, st_b, r1_b, t_b, rw_b, out_b, pre_b)

    row32 = lax.broadcasted_iota(jnp.int32, (2 * KD, TOK), 0)
    row = lax.broadcasted_iota(jnp.int32, (TOK, TOK), 0)
    col = lax.broadcasted_iota(jnp.int32, (TOK, TOK), 1)
    causal = col <= row
    frow = lax.broadcasted_iota(jnp.int32, (ROWS, TOK), 0)
    add_first = jnp.where(frow == 0, 1.0, 0.0)
    add_second = jnp.where(frow <= KD, 1.0, 0.0)
    pair_scale = 1.0 / (math.sqrt(2.0) * math.sqrt(KD))
    scale = jnp.where(frow == 0, 1.0, jnp.where(frow <= KD, 1.0 / math.sqrt(math.sqrt(KD)), pair_scale))
    weight = jnp.where(frow >= 33, 2.0, 1.0)

    def factors(x, h):
        rows = slice(h * ROWS, (h + 1) * ROWS)
        return nn(e1_ref[rows, :], x) + add_first, nn(e2_ref[rows, :], x) + add_second

    def phi(x, h):
        a, b = factors(x, h)
        return (a * b * scale).astype(BF)

    def heavy(features):
        return (features.astype(F32) * weight).astype(BF)

    def pull(x, h, cot):
        a, b = factors(x, h)
        cot = cot * (scale * weight)
        return nn(f1_ref[h], (cot * b).astype(BF)) + nn(f2_ref[h], (cot * a).astype(BF))

    def own(x, h):
        inside = (row32 >= h * KD) & (row32 < (h + 1) * KD)
        return jnp.where(inside, x.astype(F32), 0.0).astype(BF)

    cols = [slice(h * DV, (h + 1) * DV) for h in range(2)]
    ql, kl = ql_ref[...], kl_ref[...]

    for h in range(2):
        key_phi = phi(kl, h)
        phik_sc[h] = key_phi
        fwd.put(h, nn(key_phi, v_ref[:, cols[h]]))

    pl.semaphore_wait(barrier, len(peers))
    for j in (2, 6):
        pl.semaphore_signal(far, inc=1, device_id=at(group + j, member), device_id_type=MESH)
    fwd.start()

    def lin_score(h):
        return tn(own(ql, h), kl) * (1.0 / math.sqrt(KD))

    for h in range(2):
        phiq_sc[h] = phi(ql, h)
        s = lin_score(h)
        ker = jnp.where(causal, 1.0 + s + 0.5 * s * s, 0.0).astype(BF)
        ker_sc[h] = ker
        lin_sc[:, cols[h]] = nn(ker, v_ref[:, cols[h]])

    pl.semaphore_wait(far, 2)
    fwd.groups()
    rim = [
        send(wk_ref, krim, 42, ahead),
        send(v_ref, vrim, 43, ahead),
    ]

    scale_win = 1.0 / math.sqrt(WD)
    edge = (col > row) & (ctx > 0)
    wait_all(rim)

    def window(h):
        c = cols[h]
        q, k1, k2 = wq_ref[:, c], krim[:, c], wk_ref[:, c]
        v1, v2, do = vrim[:, c], v_ref[:, c], do_ref[:, c]
        s1 = jnp.where(edge, nt(q, k1) * scale_win, -1e30)
        s2 = jnp.where(causal, nt(q, k2) * scale_win, -1e30)
        top = jnp.maximum(
            jnp.max(s1, axis=1, keepdims=True), jnp.max(s2, axis=1, keepdims=True)
        )
        x1 = jnp.where(edge, jnp.exp(s1 - top), 0.0)
        x2 = jnp.where(causal, jnp.exp(s2 - top), 0.0)
        inv = 1.0 / (jnp.sum(x1, axis=1, keepdims=True) + jnp.sum(x2, axis=1, keepdims=True))
        p1, p2 = x1 * inv, x2 * inv
        b1, b2 = p1.astype(BF), p2.astype(BF)
        out = nn(b1, v1) + nn(b2, v2)
        win_sc[:, c] = out
        delta = jnp.sum(do.astype(F32) * out, axis=1, keepdims=True)
        g1 = (p1 * (nt(do, v1) - delta)).astype(BF)
        g2 = (p2 * (nt(do, v2) - delta)).astype(BF)
        gkout[:, c] = (tn(g1, q) * scale_win).astype(BF)
        gvout[:, c] = tn(b1, do).astype(BF)
        gwq_ref[:, c] = ((nn(g1, k1) + nn(g2, k2)) * scale_win).astype(BF)
        gkacc[:, c] = tn(g2, q) * scale_win
        gvacc[:, c] = tn(b2, do)

    window(0)
    fwd.spread()
    window(1)
    fwd.finish()

    gain = gain_ref[...]
    for h in range(2):
        prefix = fwd.state(h)
        lin_sc[:, cols[h]] += tn(heavy(phiq_sc[h]), prefix)
    lin = lin_sc[...]
    gd = gain * do_ref[...].astype(F32)
    square = jnp.sum(lin * lin, axis=1, keepdims=True)
    cross = jnp.sum(gd * lin, axis=1, keepdims=True)
    both = jnp.where(col == 0, square, jnp.where(col == 1, cross, 0.0))
    sums[...] = both.T[:8]
    shares = [
        send(sums, sums_in.at[d - 1], 45 + d, {"head": lax.rem(head + d, NH)})
        for d in range(1, NH)
    ]
    back = [
        send(gkout, gkin, 44, behind),
        send(gvout, gvin, 45, behind),
    ]
    wait_all(shares)
    total = sums[...]
    for d in range(NH - 1):
        total = total + sums_in[d]
    total = jnp.concatenate([total, jnp.zeros((TOK - 8, TOK), F32)], axis=0).T
    square = jnp.sum(jnp.where(col == 0, total, 0.0), axis=1, keepdims=True)
    cross = jnp.sum(jnp.where(col == 1, total, 0.0), axis=1, keepdims=True)
    inverse = 1.0 / jnp.sqrt(square * (1.0 / WIDTH) + EPS)
    grad_lin = (
        inverse * gd - lin * (inverse * inverse * inverse * (cross * (1.0 / WIDTH)))
    ).astype(BF)
    for h in range(2):
        bwd.put(h, nn(phiq_sc[h], grad_lin[:, cols[h]]))
    bwd.start()
    mixed_ref[...] = (lin * inverse * gain + win_sc[...]).astype(BF)

    gq = jnp.zeros((2 * KD, TOK), F32)
    gk = jnp.zeros((2 * KD, TOK), F32)
    for h in range(2):
        gl = grad_lin[:, cols[h]]
        g = nt(gl, v_ref[:, cols[h]]) * (1.0 + lin_score(h))
        g = jnp.where(causal, g, 0.0).astype(BF)
        gq = gq + nt(own(kl, h), g) * (1.0 / math.sqrt(KD))
        gk = gk + nn(own(ql, h), g) * (1.0 / math.sqrt(KD))
    bwd.groups()
    for h in range(2):
        gl = grad_lin[:, cols[h]]
        prefix = fwd.state(h)
        gq = gq + pull(ql, h, nt(prefix, gl))
        gvacc[:, cols[h]] += tn(ker_sc[h], gl)
    gql_ref[...] = gq.astype(BF)
    bwd.spread()
    wait_all(back)
    gwk_ref[...] = (gkacc[...] + gkin[...].astype(F32)).astype(BF)
    gvacc[...] += gvin[...].astype(F32)
    leaves = [
        pltpu.make_async_copy(source, target, leave.at[i])
        for i, (source, target) in enumerate(
            ((mixed_ref, mixed_out), (gql_ref, gql_out), (gwq_ref, gwq_out),
             (gwk_ref, gwk_out), (gv_ref, gv_out), (gkl_ref, gkl_out))
        )
    ]
    for copy in leaves[:4]:
        copy.start()
    bwd.finish()
    for h in range(2):
        suffix = bwd.state(h)
        gv_ref[:, cols[h]] = (gvacc[:, cols[h]] + tn(heavy(phik_sc[h]), suffix)).astype(BF)
        gk = gk + pull(kl, h, nt(suffix, v_ref[:, cols[h]]))
    leaves[4].start()
    gkl_ref[...] = gk.astype(BF)
    leaves[5].start()
    for copy in leaves:
        copy.wait()
    for copy in sends:
        copy.wait_send()
    for copy, sent, _ in fwd.c2 + bwd.c2:
        pl.when(sent)(copy.wait_send)


def shards(query_lin, key_lin, values, win_queries, win_keys, gain, grad_out):
    first, second = selectors()
    wide = jax.ShapeDtypeStruct((TOK, 2 * DV), BF)
    thin = jax.ShapeDtypeStruct((2 * KD, TOK), BF)
    full = pltpu.VMEM((TOK, 2 * DV), BF)
    full32 = pltpu.VMEM((TOK, 2 * DV), F32)
    one = pltpu.VMEM((SLICE, DV), BF)
    three = pltpu.VMEM((GROUPS - 1, SLICE, DV), BF)
    every = pltpu.VMEM((GROUP, SLICE, DV), BF)
    scan = [every, every, one, three, every, every]
    outs = pl.pallas_call(
        kernel,
        out_shape=(wide, thin, thin, wide, wide, wide),
        in_specs=[pl.BlockSpec(memory_space=pl.ANY)] * 11,
        out_specs=(pl.BlockSpec(memory_space=pl.ANY),) * 6,
        scratch_shapes=[full] * 6
        + scan
        + scan
        + [
            pltpu.VMEM((8, TOK), F32),
            pltpu.VMEM((NH - 1, 8, TOK), F32),
            full32,
            full32,
            pltpu.VMEM((2, TOK, TOK), BF),
            full32,
            full32,
            pltpu.VMEM((2, ROWS, TOK), BF),
            pltpu.VMEM((2, ROWS, TOK), BF),
            pltpu.SemaphoreType.DMA((53,)),
            pltpu.SemaphoreType.DMA((53,)),
            pltpu.VMEM((2 * KD, TOK), BF),
            pltpu.VMEM((2 * KD, TOK), BF),
            full,
            full,
            full,
            pltpu.VMEM((1, 2 * DV), F32),
            full,
            pltpu.VMEM((2 * ROWS, 2 * KD), BF),
            pltpu.VMEM((2 * ROWS, 2 * KD), BF),
            pltpu.VMEM((2, 2 * KD, ROWS), BF),
            pltpu.VMEM((2, 2 * KD, ROWS), BF),
            pltpu.SemaphoreType.DMA((11,)),
            pltpu.SemaphoreType.REGULAR,
            pltpu.SemaphoreType.DMA((6,)),
            full,
            pltpu.VMEM((2 * KD, TOK), BF),
            pltpu.VMEM((2 * KD, TOK), BF),
            full,
            full,
            full,
        ],
        compiler_params=pltpu.CompilerParams(collective_id=0, has_side_effects=True),
    )(
        query_lin.T, key_lin.T, values, win_queries, win_keys, gain.reshape(1, -1), grad_out,
        jnp.asarray(first, BF), jnp.asarray(second, BF),
        jnp.asarray(turned(first), BF), jnp.asarray(turned(second), BF),
    )
    def forward(*refs):
        gets = [pltpu.make_async_copy(refs[i], refs[12 + i], refs[18].at[i]) for i in range(6)]
        puts = [pltpu.make_async_copy(refs[12 + i], refs[6 + i], refs[19].at[i]) for i in range(6)]
        for get in gets:
            get.start()
        for get, put in zip(gets, puts):
            get.wait()
            put.start()
        for put in puts:
            put.wait()

    slim = pltpu.VMEM((2 * KD, TOK), BF)
    anywhere = pl.BlockSpec(memory_space=pl.ANY)
    outs = pl.pallas_call(
        forward,
        out_shape=(wide, thin, thin, wide, wide, wide),
        in_specs=[anywhere] * 6,
        out_specs=(anywhere,) * 6,
        scratch_shapes=[
            full, slim, slim, full, full, full,
            pltpu.SemaphoreType.DMA((6,)),
            pltpu.SemaphoreType.DMA((6,)),
        ],
    )(*outs)
    return outs[0], outs[1].T, outs[2].T, outs[3], outs[4], outs[5]


def solution(mesh):
    tiled = P("ctx", "head")
    return jax.shard_map(
        shards,
        mesh=mesh,
        in_specs=(tiled, tiled, tiled, tiled, tiled, P("head"), tiled),
        out_specs=(tiled,) * 6,
        check_vma=False,
    )
```

```python
import math

import jax
import jax.numpy as jnp
import numpy as np
from jax import lax
from jax.experimental import pallas as pl
from jax.experimental.pallas import tpu as pltpu
from jax.sharding import PartitionSpec as P

HEADS = 16
KD = 16
DV = 128
WD = 128
TOK = 128
GROUP = 8
GROUPS = 8
FAR_FIRST = (4, 3, 5, 2, 6, 1, 7)
ROUND = (2, 6, 3, 5, 1, 7, 4)
NH = 8
ROWS = 160
SLICE = 2 * ROWS // GROUP
PER = GROUP // 2
WIDTH = HEADS * DV
EPS = 1e-06
MESH = pl.DeviceIdType.MESH
BF = jnp.bfloat16
F32 = jnp.float32


def selectors():
    first = np.zeros((2 * ROWS, 2 * KD), np.float32)
    second = np.zeros((2 * ROWS, 2 * KD), np.float32)
    for h in range(2):
        base, lane = h * ROWS, h * KD
        for i in range(KD):
            first[base + 1 + i, lane + i] = 1
            first[base + 17 + i, lane + i] = 1
            second[base + 17 + i, lane + i] = 1
        row = base + 33
        for i in range(KD):
            for j in range(i + 1, KD):
                first[row, lane + i] = 1
                second[row, lane + j] = 1
                row += 1
    return first, second


def turned(table):
    return table.reshape(2, ROWS, 2 * KD).transpose(0, 2, 1)


def nn(a, b):
    return lax.dot_general(a, b, (((1,), (0,)), ((), ())), preferred_element_type=F32)


def nt(a, b):
    return lax.dot_general(a, b, (((1,), (1,)), ((), ())), preferred_element_type=F32)


def tn(a, b):
    return lax.dot_general(a, b, (((0,), (0,)), ((), ())), preferred_element_type=F32)


def kernel(
    ql_in, kl_in, v_in, wq_in, wk_in, gain_in, do_in, e1_in, e2_in, f1_in, f2_in,
    mixed_out, gql_out, gkl_out, gv_out, gwq_out, gwk_out,
    krim, vrim, gkout, gvout, gkin, gvin,
    st_a, r1_a, t_a, rw_a, out_a, pre_a,
    st_b, r1_b, t_b, rw_b, out_b, pre_b,
    sums, sums_in, lin_sc, win_sc, ker_sc, gvacc, gkacc, phiq_sc, phik_sc,
    ss, rs,
    ql_ref, kl_ref, v_ref, wq_ref, wk_ref, gain_ref, do_ref, e1_ref, e2_ref, f1_ref, f2_ref,
    local, far, leave, mixed_ref, gql_ref, gkl_ref, gv_ref, gwq_ref, gwk_ref,
):
    ctx = lax.axis_index("ctx")
    head = lax.axis_index("head")
    group = ctx // GROUP
    member = lax.rem(ctx, GROUP)
    sends = []

    def partner(d):
        return lax.rem(member + d, GROUP)

    def at(g, m):
        return {"ctx": lax.rem(g, GROUPS) * GROUP + lax.rem(m, GROUP)}

    count = GROUP * GROUPS
    ahead = {"ctx": lax.rem(ctx + 1, count)}
    behind = {"ctx": lax.rem(ctx + count - 1, count)}

    rw_a[...] = jnp.zeros_like(rw_a)
    rw_b[...] = jnp.zeros_like(rw_b)

    barrier = pltpu.get_barrier_semaphore()
    peers = [at(group + j, member) for j in (2, 6)]
    peers += [at(group, member + d) for d in ROUND]
    peers += [at(group + j, member) for j in (1, 7)]
    peers += [ahead, behind]
    peers += [{"head": lax.rem(head + d, NH)} for d in range(1, NH)]
    for peer in peers:
        pl.semaphore_signal(barrier, inc=1, device_id=peer, device_id_type=MESH)

    inputs = (kl_in, e1_in, e2_in, v_in, ql_in, wk_in, wq_in, do_in, gain_in, f1_in, f2_in)
    held = (kl_ref, e1_ref, e2_ref, v_ref, ql_ref, wk_ref, wq_ref, do_ref, gain_ref, f1_ref, f2_ref)
    fetches = [
        pltpu.make_async_copy(source, target, local.at[i])
        for i, (source, target) in enumerate(zip(inputs, held))
    ]
    for fetch in fetches:
        fetch.start()
    for fetch in fetches:
        fetch.wait()

    def send(src, dst, slot, device):
        copy = pltpu.make_async_remote_copy(
            src_ref=src, dst_ref=dst, send_sem=ss.at[slot], recv_sem=rs.at[slot],
            device_id=device, device_id_type=MESH,
        )
        copy.start()
        sends.append(copy)
        return copy

    def wait_all(copies):
        for copy in copies:
            copy.wait_recv()

    class Scan:
        def __init__(self, sign, base, st, r1, t, rw, out, pre):
            self.sign, self.base = sign, base
            self.st, self.r1, self.t, self.rw, self.out, self.pre = st, r1, t, rw, out, pre

        def start(self):
            self.c1 = [
                send(self.st.at[partner(d)], self.r1.at[member], self.base + d - 1, at(group, member + d))
                for d in ROUND
            ]
            self.r1[member] = self.st[member]

        def groups(self):
            wait_all(self.c1)
            total = self.r1[0].astype(F32)
            for k in range(1, GROUP):
                total = total + self.r1[k].astype(F32)
            self.t[...] = total.astype(BF)
            self.c2 = []
            for j in FAR_FIRST:
                copy = pltpu.make_async_remote_copy(
                    src_ref=self.t, dst_ref=self.rw.at[j - 1],
                    send_sem=ss.at[self.base + 6 + j], recv_sem=rs.at[self.base + 6 + j],
                    device_id=at(group + j, member), device_id_type=MESH,
                )
                up = group + j < GROUPS
                sent = up if self.sign > 0 else group + j >= GROUPS
                got = group >= j if self.sign > 0 else group < j
                pl.when(sent)(copy.start)
                self.c2.append((copy, sent, got))

        def spread(self):
            for copy, _, got in self.c2:
                pl.when(got)(copy.wait_recv)
            total = self.rw[0].astype(F32)
            for j in range(1, GROUPS - 1):
                total = total + self.rw[j].astype(F32)
            order = range(GROUP) if self.sign > 0 else range(GROUP - 1, -1, -1)
            for k in order:
                self.out[k] = total.astype(BF)
                total = total + self.r1[k].astype(F32)
            self.c3 = [
                send(self.out.at[partner(d)], self.pre.at[member], self.base + 13 + d, at(group, member + d))
                for d in ROUND
            ]
            self.pre[member] = self.out[member]

        def finish(self):
            wait_all(self.c3)

        def state(self, h):
            rows = [self.pre[PER * h + k].astype(F32) for k in range(PER)]
            return jnp.concatenate(rows, axis=0).astype(BF)

        def put(self, h, state):
            for k in range(PER):
                self.st[PER * h + k] = state[k * SLICE : (k + 1) * SLICE].astype(BF)

    fwd = Scan(1, 0, st_a, r1_a, t_a, rw_a, out_a, pre_a)
    bwd = Scan(-1, 21, st_b, r1_b, t_b, rw_b, out_b, pre_b)

    row32 = lax.broadcasted_iota(jnp.int32, (2 * KD, TOK), 0)
    row = lax.broadcasted_iota(jnp.int32, (TOK, TOK), 0)
    col = lax.broadcasted_iota(jnp.int32, (TOK, TOK), 1)
    causal = col <= row
    frow = lax.broadcasted_iota(jnp.int32, (ROWS, TOK), 0)
    add_first = jnp.where(frow == 0, 1.0, 0.0)
    add_second = jnp.where(frow <= KD, 1.0, 0.0)
    pair_scale = 1.0 / (math.sqrt(2.0) * math.sqrt(KD))
    scale = jnp.where(frow == 0, 1.0, jnp.where(frow <= KD, 1.0 / math.sqrt(math.sqrt(KD)), pair_scale))
    weight = jnp.where(frow >= 33, 2.0, 1.0)

    def factors(x, h):
        rows = slice(h * ROWS, (h + 1) * ROWS)
        return nn(e1_ref[rows, :], x) + add_first, nn(e2_ref[rows, :], x) + add_second

    def phi(x, h):
        a, b = factors(x, h)
        return (a * b * scale).astype(BF)

    def heavy(features):
        return (features.astype(F32) * weight).astype(BF)

    def pull(x, h, cot):
        a, b = factors(x, h)
        cot = cot * (scale * weight)
        return nn(f1_ref[h], (cot * b).astype(BF)) + nn(f2_ref[h], (cot * a).astype(BF))

    def own(x, h):
        inside = (row32 >= h * KD) & (row32 < (h + 1) * KD)
        return jnp.where(inside, x.astype(F32), 0.0).astype(BF)

    cols = [slice(h * DV, (h + 1) * DV) for h in range(2)]
    ql, kl = ql_ref[...], kl_ref[...]

    for h in range(2):
        key_phi = phi(kl, h)
        phik_sc[h] = key_phi
        fwd.put(h, nn(key_phi, v_ref[:, cols[h]]))

    pl.semaphore_wait(barrier, len(peers))
    for j in (2, 6):
        pl.semaphore_signal(far, inc=1, device_id=at(group + j, member), device_id_type=MESH)
    fwd.start()
    rim = [
        send(wk_ref, krim, 42, ahead),
        send(v_ref, vrim, 43, ahead),
    ]

    def lin_score(h):
        return tn(own(ql, h), kl) * (1.0 / math.sqrt(KD))

    for h in range(2):
        phiq_sc[h] = phi(ql, h)
        s = lin_score(h)
        ker = jnp.where(causal, 1.0 + s + 0.5 * s * s, 0.0).astype(BF)
        ker_sc[h] = ker
        lin_sc[:, cols[h]] = nn(ker, v_ref[:, cols[h]])

    pl.semaphore_wait(far, 2)
    fwd.groups()

    scale_win = 1.0 / math.sqrt(WD)
    edge = (col > row) & (ctx > 0)
    wait_all(rim)

    def window(h):
        c = cols[h]
        q, k1, k2 = wq_ref[:, c], krim[:, c], wk_ref[:, c]
        v1, v2, do = vrim[:, c], v_ref[:, c], do_ref[:, c]
        s1 = jnp.where(edge, nt(q, k1) * scale_win, -1e30)
        s2 = jnp.where(causal, nt(q, k2) * scale_win, -1e30)
        top = jnp.maximum(
            jnp.max(s1, axis=1, keepdims=True), jnp.max(s2, axis=1, keepdims=True)
        )
        x1 = jnp.where(edge, jnp.exp(s1 - top), 0.0)
        x2 = jnp.where(causal, jnp.exp(s2 - top), 0.0)
        inv = 1.0 / (jnp.sum(x1, axis=1, keepdims=True) + jnp.sum(x2, axis=1, keepdims=True))
        p1, p2 = x1 * inv, x2 * inv
        b1, b2 = p1.astype(BF), p2.astype(BF)
        out = nn(b1, v1) + nn(b2, v2)
        win_sc[:, c] = out
        delta = jnp.sum(do.astype(F32) * out, axis=1, keepdims=True)
        g1 = (p1 * (nt(do, v1) - delta)).astype(BF)
        g2 = (p2 * (nt(do, v2) - delta)).astype(BF)
        gkout[:, c] = (tn(g1, q) * scale_win).astype(BF)
        gvout[:, c] = tn(b1, do).astype(BF)
        gwq_ref[:, c] = ((nn(g1, k1) + nn(g2, k2)) * scale_win).astype(BF)
        gkacc[:, c] = tn(g2, q) * scale_win
        gvacc[:, c] = tn(b2, do)

    window(0)
    fwd.spread()
    window(1)
    fwd.finish()

    gain = gain_ref[...]
    for h in range(2):
        prefix = fwd.state(h)
        lin_sc[:, cols[h]] += tn(heavy(phiq_sc[h]), prefix)
    lin = lin_sc[...]
    gd = gain * do_ref[...].astype(F32)
    square = jnp.sum(lin * lin, axis=1, keepdims=True)
    cross = jnp.sum(gd * lin, axis=1, keepdims=True)
    both = jnp.where(col == 0, square, jnp.where(col == 1, cross, 0.0))
    sums[...] = both.T[:8]
    shares = [
        send(sums, sums_in.at[d - 1], 45 + d, {"head": lax.rem(head + d, NH)})
        for d in range(1, NH)
    ]
    back = [
        send(gkout, gkin, 44, behind),
        send(gvout, gvin, 45, behind),
    ]
    wait_all(shares)
    total = sums[...]
    for d in range(NH - 1):
        total = total + sums_in[d]
    total = jnp.concatenate([total, jnp.zeros((TOK - 8, TOK), F32)], axis=0).T
    square = jnp.sum(jnp.where(col == 0, total, 0.0), axis=1, keepdims=True)
    cross = jnp.sum(jnp.where(col == 1, total, 0.0), axis=1, keepdims=True)
    inverse = 1.0 / jnp.sqrt(square * (1.0 / WIDTH) + EPS)
    grad_lin = (
        inverse * gd - lin * (inverse * inverse * inverse * (cross * (1.0 / WIDTH)))
    ).astype(BF)
    for h in range(2):
        bwd.put(h, nn(phiq_sc[h], grad_lin[:, cols[h]]))
    bwd.start()
    mixed_ref[...] = (lin * inverse * gain + win_sc[...]).astype(BF)

    gq = jnp.zeros((2 * KD, TOK), F32)
    gk = jnp.zeros((2 * KD, TOK), F32)
    for h in range(2):
        gl = grad_lin[:, cols[h]]
        g = nt(gl, v_ref[:, cols[h]]) * (1.0 + lin_score(h))
        g = jnp.where(causal, g, 0.0).astype(BF)
        gq = gq + nt(own(kl, h), g) * (1.0 / math.sqrt(KD))
        gk = gk + nn(own(ql, h), g) * (1.0 / math.sqrt(KD))
    bwd.groups()
    for h in range(2):
        gl = grad_lin[:, cols[h]]
        prefix = fwd.state(h)
        gq = gq + pull(ql, h, nt(prefix, gl))
        gvacc[:, cols[h]] += tn(ker_sc[h], gl)
    gql_ref[...] = gq.astype(BF)
    bwd.spread()
    wait_all(back)
    gwk_ref[...] = (gkacc[...] + gkin[...].astype(F32)).astype(BF)
    gvacc[...] += gvin[...].astype(F32)
    leaves = [
        pltpu.make_async_copy(source, target, leave.at[i])
        for i, (source, target) in enumerate(
            ((mixed_ref, mixed_out), (gql_ref, gql_out), (gwq_ref, gwq_out),
             (gwk_ref, gwk_out), (gv_ref, gv_out), (gkl_ref, gkl_out))
        )
    ]
    for copy in leaves[:4]:
        copy.start()
    bwd.finish()
    for h in range(2):
        suffix = bwd.state(h)
        gv_ref[:, cols[h]] = (gvacc[:, cols[h]] + tn(heavy(phik_sc[h]), suffix)).astype(BF)
        gk = gk + pull(kl, h, nt(suffix, v_ref[:, cols[h]]))
    leaves[4].start()
    gkl_ref[...] = gk.astype(BF)
    leaves[5].start()
    for copy in leaves:
        copy.wait()
    for copy in sends:
        copy.wait_send()
    for copy, sent, _ in fwd.c2 + bwd.c2:
        pl.when(sent)(copy.wait_send)


def shards(query_lin, key_lin, values, win_queries, win_keys, gain, grad_out):
    first, second = selectors()
    wide = jax.ShapeDtypeStruct((TOK, 2 * DV), BF)
    thin = jax.ShapeDtypeStruct((2 * KD, TOK), BF)
    full = pltpu.VMEM((TOK, 2 * DV), BF)
    full32 = pltpu.VMEM((TOK, 2 * DV), F32)
    one = pltpu.VMEM((SLICE, DV), BF)
    three = pltpu.VMEM((GROUPS - 1, SLICE, DV), BF)
    every = pltpu.VMEM((GROUP, SLICE, DV), BF)
    scan = [every, every, one, three, every, every]
    outs = pl.pallas_call(
        kernel,
        out_shape=(wide, thin, thin, wide, wide, wide),
        in_specs=[pl.BlockSpec(memory_space=pl.ANY)] * 11,
        out_specs=(pl.BlockSpec(memory_space=pl.ANY),) * 6,
        scratch_shapes=[full] * 6
        + scan
        + scan
        + [
            pltpu.VMEM((8, TOK), F32),
            pltpu.VMEM((NH - 1, 8, TOK), F32),
            full32,
            full32,
            pltpu.VMEM((2, TOK, TOK), BF),
            full32,
            full32,
            pltpu.VMEM((2, ROWS, TOK), BF),
            pltpu.VMEM((2, ROWS, TOK), BF),
            pltpu.SemaphoreType.DMA((53,)),
            pltpu.SemaphoreType.DMA((53,)),
            pltpu.VMEM((2 * KD, TOK), BF),
            pltpu.VMEM((2 * KD, TOK), BF),
            full,
            full,
            full,
            pltpu.VMEM((1, 2 * DV), F32),
            full,
            pltpu.VMEM((2 * ROWS, 2 * KD), BF),
            pltpu.VMEM((2 * ROWS, 2 * KD), BF),
            pltpu.VMEM((2, 2 * KD, ROWS), BF),
            pltpu.VMEM((2, 2 * KD, ROWS), BF),
            pltpu.SemaphoreType.DMA((11,)),
            pltpu.SemaphoreType.REGULAR,
            pltpu.SemaphoreType.DMA((6,)),
            full,
            pltpu.VMEM((2 * KD, TOK), BF),
            pltpu.VMEM((2 * KD, TOK), BF),
            full,
            full,
            full,
        ],
        compiler_params=pltpu.CompilerParams(collective_id=0, has_side_effects=True),
    )(
        query_lin.T, key_lin.T, values, win_queries, win_keys, gain.reshape(1, -1), grad_out,
        jnp.asarray(first, BF), jnp.asarray(second, BF),
        jnp.asarray(turned(first), BF), jnp.asarray(turned(second), BF),
    )
    def forward(*refs):
        gets = [pltpu.make_async_copy(refs[i], refs[12 + i], refs[18].at[i]) for i in range(6)]
        puts = [pltpu.make_async_copy(refs[12 + i], refs[6 + i], refs[19].at[i]) for i in range(6)]
        for get in gets:
            get.start()
        for get, put in zip(gets, puts):
            get.wait()
            put.start()
        for put in puts:
            put.wait()

    slim = pltpu.VMEM((2 * KD, TOK), BF)
    anywhere = pl.BlockSpec(memory_space=pl.ANY)
    outs = pl.pallas_call(
        forward,
        out_shape=(wide, thin, thin, wide, wide, wide),
        in_specs=[anywhere] * 6,
        out_specs=(anywhere,) * 6,
        scratch_shapes=[
            full, slim, slim, full, full, full,
            pltpu.SemaphoreType.DMA((6,)),
            pltpu.SemaphoreType.DMA((6,)),
        ],
    )(*outs)
    return outs[0], outs[1].T, outs[2].T, outs[3], outs[4], outs[5]


def solution(mesh):
    tiled = P("ctx", "head")
    return jax.shard_map(
        shards,
        mesh=mesh,
        in_specs=(tiled, tiled, tiled, tiled, tiled, P("head"), tiled),
        out_specs=(tiled,) * 6,
        check_vma=False,
    )
```
